32 devices in a mesh: cfg: 2 (over y), slab: 4 (over z), tile: 2 (over x), spin: 2 (over core).
Axes of the slice: x: 2, y: 2, z: 4, core: 2. Of those that a mesh axis runs over, the one named last changes fastest.
Arguments:
- eigenvectors: bfloat16 [4, 2, 3, 8, 1024, 256], P(('cfg', 'tile'), None, None, 'slab', 'spin'), parts along dimension 0, may hold values from -6 to 6
- gauge_links: float32 [4, 2, 3, 3, 8, 1024], P(('cfg', 'tile'), None, None, None, 'slab', 'spin'), parts along dimension 0, may hold values from -2.5 to 2.5
- momenta: int32 [2, 3], replicated, may hold values from -2 to 2
- displacement: int32 [2], replicated, may hold values from 1 to 2, as said below
- slice_pairs: int32 [4, 2], P('tile'), may hold values from 0 to 1, as said below
- perambulators: bfloat16 [8, 2, 1024, 1024], P(('cfg', 'tile'), None, 'spin', 'slab'), parts along dimension 0, may hold values from -6 to 6
Outputs:
- meson_blocks: bfloat16 [8, 2, 1024, 1024], P(('cfg', 'tile'), None, 'spin', 'slab'), parts along dimension 0
The draws below stay inside these ranges and needn't reach their ends.
There are 2 independent parts, one for each index of `cfg`. The reference program is written for one: setup_inputs(seed, part) draws one part's arguments, and reference() takes and returns one part's arrays. A program takes and returns all parts, laid end to end along the dimension named above; an argument that names none is the same for every part. Nothing has to cross between parts.
Inputs may be any that keep to these rules, and one draw needn't show every extreme that they name: `displacement`: the entries are 1 and 2 in some order, so one elemental is displaced forward and the other backward. `slice_pairs`: column 0 is the sink slice and column 1 the source slice; every pair of slices in 0 to 1 appears exactly once.
All inputs are finite; a program needn't handle non-finite values.
Results may differ from the reference program's by a relative error of at most 0.008.
Values may be sent and summed in bfloat16 or wider, within the bound.
No kernel may reach another device: no remote copies, remote signals or barrier semaphores. Data moves between devices by JAX's collectives and lax.ppermute only.
A program may use at most 64 MiB of HBM per device.

```python
import math
import jax
import jax.numpy as jnp
from jax import lax

NV = 256
NS = 4
ELEMS = 2
LY = 32
LZ = 32
LX = 8
NT = 2
PAIRS = 4


def draw_displacement(key, part):
    shuffled = jax.random.permutation(jax.random.fold_in(key, 7), ELEMS)
    return (1 + shuffled % 2).astype(jnp.int32)


def draw_slice_pairs(key, part):
    shuffled = jax.random.permutation(jax.random.fold_in(key, 5), PAIRS)
    return jnp.stack([shuffled // NT, shuffled % NT], axis=1).astype(jnp.int32)


def set_ends(array, stream_key, low, high):
    longest = array.shape.index(max(array.shape))
    spots = []
    for shift in (0, 1):
        where = [jax.random.randint(jax.random.fold_in(stream_key, axis), (), 0, length) for axis, length in enumerate(array.shape)]
        where[longest] = (where[longest] + shift) % array.shape[longest]
        spots.append(tuple(where))
    return array.at[spots[0]].set(low).at[spots[1]].set(high)


def levels(stream_key, shape, pieces, least, top_value):
    def one(dim, parts):
        draws = jax.random.uniform(jax.random.fold_in(jax.random.fold_in(stream_key, 6), dim), (parts,), jnp.float32, least / len(pieces), top_value / len(pieces))
        return jnp.repeat(jnp.exp(draws), shape[dim] // parts).reshape((-1,) + (1,) * (len(shape) - dim - 1))

    factor_of = one(*pieces[0])
    for cut in pieces[1:]:
        factor_of = factor_of * one(*cut)
    return factor_of


def bell_draw(own_key, extent, width, reach, shards=(), kind=jnp.bfloat16):
    gain = levels(own_key, extent, shards, -0.22, 0.18) if shards else 1.0
    values = jax.random.normal(own_key, extent, jnp.float32) * width * gain
    return jnp.minimum(jnp.maximum(values, -reach), reach).astype(kind)


def setup_inputs(seed: int = 0, part: int = 0) -> dict:
    seeds = jax.random.split(jax.random.key(seed), 7)
    part_keys = jax.random.split(jax.random.fold_in(seeds[6], part), 7)
    return {
        "eigenvectors": bell_draw(part_keys[0], (NT, 2, 3, LX, LY * LZ, NV), 1.0, 6.0, ((0, 2), (3, 4), (4, 2))),
        "gauge_links": bell_draw(part_keys[1], (NT, 2, 3, 3, LX, LY * LZ), 0.408, 2.5, ((0, 2), (4, 4), (5, 2)), jnp.float32),
        "momenta": set_ends(jax.random.randint(seeds[2], (ELEMS, 3), -2, 3), jax.random.fold_in(seeds[2], 1), -2, 2).astype(jnp.int32),
        "displacement": draw_displacement(jax.random.fold_in(seeds[6], 71), part),
        "slice_pairs": draw_slice_pairs(jax.random.fold_in(seeds[6], 71), part),
        "perambulators": bell_draw(part_keys[5], (PAIRS, 2, NS * NV, NS * NV), 1.0, 6.0, ((0, 2), (2, 2), (3, 4))),
    }


def color_apply(link_field, vectors_here, adjoint):
    field_real = vectors_here[0].astype(jnp.float32)
    field_imag = vectors_here[1].astype(jnp.float32)
    if adjoint:
        link_real = jnp.swapaxes(link_field[0], 0, 1)
        link_imag = -jnp.swapaxes(link_field[1], 0, 1)
    else:
        link_real = link_field[0]
        link_imag = link_field[1]
    out_real = jnp.zeros(field_real.shape, jnp.float32)
    out_imag = jnp.zeros(field_real.shape, jnp.float32)
    for color_in in range(3):
        column_real = link_real[:, color_in][:, :, :, None]
        column_imag = link_imag[:, color_in][:, :, :, None]
        out_real = out_real + column_real * field_real[color_in] - column_imag * field_imag[color_in]
        out_imag = out_imag + column_real * field_imag[color_in] + column_imag * field_real[color_in]
    return jnp.stack([out_real, out_imag])

def phase_table(momenta, x_global, yz_global, extent_x, extent_y, extent_z):
    y_coord = yz_global // extent_z
    z_coord = yz_global % extent_z
    wave_x = jnp.mod(momenta[:, 0:1] * x_global[None, :], extent_x)
    wave_y = jnp.mod(momenta[:, 1:2] * y_coord[None, :], extent_y)
    wave_z = jnp.mod(momenta[:, 2:3] * z_coord[None, :], extent_z)
    numerator = wave_x[:, :, None] * (extent_y * extent_z) + (wave_y * (extent_x * extent_z) + wave_z * (extent_x * extent_y))[:, None, :]
    angle = numerator.astype(jnp.float32) * (2.0 * math.pi / (extent_x * extent_y * extent_z))
    return (jnp.cos(angle), -jnp.sin(angle))

def elemental_terms(vectors_here, forward, backward, rot_real, rot_imag, displacement):
    vector_count = vectors_here.shape[-1]
    field_real = vectors_here[0].reshape(-1, vector_count)
    field_imag = vectors_here[1].reshape(-1, vector_count)
    tops = []
    bottoms = []
    for which in range(displacement.shape[0]):
        forward_mask = (displacement[which] == 1).astype(jnp.float32)
        moved_real = forward_mask * forward[0] + (1.0 - forward_mask) * backward[0]
        moved_imag = forward_mask * forward[1] + (1.0 - forward_mask) * backward[1]
        cosine = rot_real[which][None, :, :, None]
        sine = rot_imag[which][None, :, :, None]
        phased_real = (cosine * moved_real - sine * moved_imag).astype(jnp.bfloat16).reshape(-1, vector_count)
        phased_imag = (cosine * moved_imag + sine * moved_real).astype(jnp.bfloat16).reshape(-1, vector_count)
        tops += [phased_real, phased_imag]
        bottoms += [phased_imag, -phased_real]
    top_block = jnp.concatenate(tops, axis=1)
    bottom_block = jnp.concatenate(bottoms, axis=1)
    numbers = (((0,), (0,)), ((), ()))
    first = lax.dot_general(field_real, top_block, numbers, preferred_element_type=jnp.float32)
    second = lax.dot_general(field_imag, bottom_block, numbers, preferred_element_type=jnp.float32)
    return first + second

def reference(eigenvectors, gauge_links, momenta, displacement, slice_pairs, perambulators):
    normalize = 1.0 / math.sqrt(3072 * LX * LY * LZ)
    yz_global = jnp.arange(LY * LZ, dtype=jnp.int32)

    def one_slice(slice_args):
        field_all, link_all = slice_args

        def plane_step(carry, plane_index):
            after = ((plane_index + 1) % LX).astype(jnp.int32)
            before = ((plane_index + LX - 1) % LX).astype(jnp.int32)
            here = lax.dynamic_slice_in_dim(field_all, plane_index, 1, 2)
            ahead = lax.dynamic_slice_in_dim(field_all, after, 1, 2)
            behind = lax.dynamic_slice_in_dim(field_all, before, 1, 2)
            link_here = lax.dynamic_slice_in_dim(link_all, plane_index, 1, 3)
            link_behind = lax.dynamic_slice_in_dim(link_all, before, 1, 3)
            forward = color_apply(link_here, ahead, False)
            back_local = lax.optimization_barrier(color_apply(link_behind, behind, True).astype(jnp.bfloat16))
            backward = back_local.astype(jnp.float32)
            rot_real, rot_imag = phase_table(momenta, plane_index[None], yz_global, LX, LY, LZ)
            return (carry + elemental_terms(here, forward, backward, rot_real, rot_imag, displacement), None)
        start_sum = jnp.zeros((NV, 4 * NV), jnp.float32)
        summed, _ = lax.scan(plane_step, start_sum, jnp.arange(LX, dtype=jnp.int32))
        return (summed * normalize).astype(jnp.bfloat16)
    elemental_table = lax.map(one_slice, (eigenvectors, gauge_links))

    def one_pair(pair_args):
        pair_row, block = pair_args
        sink = lax.dynamic_index_in_dim(elemental_table, pair_row[0], 0, keepdims=False).astype(jnp.float32)
        source = lax.dynamic_index_in_dim(elemental_table, pair_row[1], 0, keepdims=False).astype(jnp.float32)
        sink_real = sink[:, :NV]
        sink_imag = sink[:, NV:2 * NV]
        source_real = source[:, 2 * NV:3 * NV]
        source_imag = source[:, 3 * NV:]
        block_real = block[0].astype(jnp.float32).reshape(NS, NV, NS * NV)
        block_imag = block[1].astype(jnp.float32).reshape(NS, NV, NS * NV)
        left_real = jnp.einsum('vu,suj->svj', sink_real, block_real) - jnp.einsum('vu,suj->svj', sink_imag, block_imag)
        left_imag = jnp.einsum('vu,suj->svj', sink_real, block_imag) + jnp.einsum('vu,suj->svj', sink_imag, block_real)
        left_block = jnp.stack([left_real, left_imag]).reshape(2, NS * NV, NV, NS)
        left_block = lax.optimization_barrier(left_block.astype(jnp.bfloat16)).astype(jnp.float32)
        out_real = jnp.einsum('rvs,vw->rws', left_block[0], source_real) - jnp.einsum('rvs,vw->rws', left_block[1], source_imag)
        out_imag = jnp.einsum('rvs,vw->rws', left_block[0], source_imag) + jnp.einsum('rvs,vw->rws', left_block[1], source_real)
        return jnp.stack([out_real, out_imag]).reshape(2, NS * NV, NV * NS).astype(jnp.bfloat16)
    return lax.map(one_pair, (slice_pairs, perambulators))
```

```python
import functools
import math

import jax
import jax.numpy as jnp
from jax import lax
from jax.experimental import pallas as pl
from jax.experimental.pallas import tpu as pltpu
from jax.sharding import PartitionSpec as P

NS = 4
LY = 32
LZ = 32
COLORS = 3
COEFS = 24


def shift(x, axis, by):
    count = lax.axis_size(axis)
    return lax.ppermute(x, axis, [(i, (i + by) % count) for i in range(count)])


def swap(x, axis, distance):
    count = lax.axis_size(axis)
    return lax.ppermute(x, axis, [(i, i ^ distance) for i in range(count)])


def vmem():
    return pl.BlockSpec(memory_space=pltpu.VMEM)


def smem():
    return pl.BlockSpec(memory_space=pltpu.SMEM)


def field_kernel(fields_ref, coefs_ref, inner_ref, outer_ref, rotated):
    planes, block, vectors = fields_ref.shape[2:]
    tile = 16

    @pl.when(pl.program_id(0) == 0)
    def _():
        inner_ref[...] = jnp.zeros_like(inner_ref)

    for plane in range(planes):

        def rows_step(step, carry):
            rows = pl.ds(pl.multiple_of(step * tile, tile), tile)
            coefs = coefs_ref[plane, rows, :]

            def coef(which):
                return coefs[:, which : which + 1]

            real = [fields_ref[0, c, plane, rows, :].astype(jnp.float32) for c in range(COLORS)]
            imag = [fields_ref[1, c, plane, rows, :].astype(jnp.float32) for c in range(COLORS)]
            for out in range(COLORS):
                local_real = None
                for c in range(COLORS):
                    link_real = coef(COLORS * c + out)
                    link_imag = coef(COLORS * COLORS + COLORS * c + out)
                    term_real = link_real * real[c] + link_imag * imag[c]
                    term_imag = link_real * imag[c] - link_imag * real[c]
                    local_real = term_real if local_real is None else local_real + term_real
                    local_imag = term_imag if c == 0 else local_imag + term_imag
                for slot in range(2):
                    turn_real = coef(2 * COLORS * COLORS + 2 * slot)
                    turn_imag = coef(2 * COLORS * COLORS + 2 * slot + 1)
                    at = 2 * slot * vectors
                    rotated[out, rows, at : at + vectors] = (
                        turn_real * local_real - turn_imag * local_imag
                    ).astype(jnp.bfloat16)
                    at += vectors
                    rotated[out, rows, at : at + vectors] = (
                        turn_real * local_imag + turn_imag * local_real
                    ).astype(jnp.bfloat16)
            return carry

        lax.fori_loop(0, block // tile, rows_step, 0)
        for c in range(COLORS):
            if plane + 1 < planes:
                ahead = jnp.concatenate(
                    [fields_ref[0, c, plane + 1], fields_ref[1, c, plane + 1]], axis=1
                )
                inner_ref[...] += lax.dot_general(
                    rotated[c], ahead, (((0,), (0,)), ((), ())), preferred_element_type=jnp.float32
                )
            else:
                outer_ref[c] = rotated[c].T


def rim_kernel(normalize, meta_ref, outer_ref, inner_ref, rim_ref, keep_ref, send_ref):
    vectors = rim_ref.shape[-1]
    for slot, out in ((1, send_ref), (0, keep_ref)):
        at = 2 * slot * vectors
        totals = []
        for part in range(2):
            total = inner_ref[at : at + 2 * vectors, part * vectors : (part + 1) * vectors]
            for c in range(COLORS):
                total = total + jnp.dot(
                    outer_ref[c, at : at + 2 * vectors, :],
                    rim_ref[part, c],
                    preferred_element_type=jnp.float32,
                )
            totals.append(total)
        real = totals[0][:vectors] + totals[1][vectors:]
        imag = totals[0][vectors:] - totals[1][:vectors]
        out[meta_ref[1]] = (real * normalize).astype(out.dtype)
        out[1 - meta_ref[1]] = (imag * normalize).astype(out.dtype)


def deal_kernel(share, meta_ref, perams_ref, *outs):
    spin_rows, vectors, width = perams_ref.shape[2:]
    per = width // NS
    source = lax.broadcasted_iota(jnp.int32, (width, width), 0)
    target = lax.broadcasted_iota(jnp.int32, (width, width), 1)
    move = (target == (source % NS) * per + source // NS).astype(jnp.float32)
    move = move.astype(jnp.bfloat16)
    for by, out in enumerate(outs):
        item = (meta_ref[4] ^ by) // share
        for part in range(2):
            out[part] = jnp.dot(
                perams_ref[item // spin_rows, part, lax.rem(item, spin_rows)],
                move,
                preferred_element_type=jnp.float32,
            ).astype(jnp.bfloat16)


def block_kernel(slab, share, meta_ref, *refs):
    parts = refs[:4]
    chunks = refs[4 : 4 + slab]
    outs = refs[4 + slab : -2]
    table_ref, turned_ref = refs[-2:]
    vectors = parts[0].shape[0]
    per = vectors // slab
    core, parity, place = meta_ref[0], meta_ref[1], meta_ref[4]
    found = [piece[...].astype(jnp.float32) for piece in parts]

    def pick(elem):
        mine = core == elem
        first = jnp.where(mine, found[0], found[2])
        second = jnp.where(mine, found[1], found[3])
        real = jnp.where(parity == 0, first, second)
        imag = jnp.where(parity == 0, second, first)
        forward = meta_ref[5 + elem] == 1
        return (
            jnp.where(forward, real, real.T),
            jnp.where(forward, -imag, imag.T),
        )

    real, imag = pick(0)
    real, imag = real.astype(jnp.bfloat16), imag.astype(jnp.bfloat16)
    matrix = jnp.concatenate(
        [jnp.concatenate([real, -imag], axis=1), jnp.concatenate([imag, real], axis=1)], axis=0
    )
    columns = []
    for spin in range(NS):
        at = spin * per
        columns += [
            chunk[...].reshape(2 * vectors, NS * per)[:, at : at + per] for chunk in chunks
        ]
    spread = jnp.concatenate(columns, axis=1)
    left = jnp.dot(matrix, spread, preferred_element_type=jnp.float32).astype(jnp.bfloat16)
    width = vectors // share
    count = slab // share
    lane = lax.broadcasted_iota(jnp.int32, (per, width), 1) // per
    for part, value in enumerate(pick(1)):
        table_ref[...] = value
        for chunk in range(slab):
            row = pl.multiple_of((place ^ chunk) * per, per)
            rows = table_ref[pl.ds(row, per), :]
            turned = rows[:, :width]
            for group in range(1, share):
                turned = jnp.where(
                    lax.rem(place, share) == group,
                    rows[:, group * width : (group + 1) * width],
                    turned,
                )
            step = 1
            while step < count:
                down = pltpu.roll(turned, step * per, 1)
                up = pltpu.roll(turned, width - step * per, 1)
                moved = jnp.where((lane // step) % 2 == 0, up, down)
                turned = jnp.where((place // (share * step)) % 2 == 1, moved, turned)
                step *= 2
            turned_ref[chunk * per : (chunk + 1) * per, part * width : (part + 1) * width] = (
                turned
            )
    right = turned_ref[...].astype(jnp.bfloat16)
    reals, imags = [], []
    for spin in range(NS):
        both = jnp.dot(
            left[:, spin * vectors : (spin + 1) * vectors],
            right,
            preferred_element_type=jnp.float32,
        )
        reals.append(both[:vectors, :width] - both[vectors:, width:])
        imags.append(both[:vectors, width:] + both[vectors:, :width])
    for which, out in enumerate(outs):
        at = which * per
        for part, values in ((0, reals), (1, imags)):
            out[part] = jnp.concatenate(
                [value[:, at : at + per] for value in values], axis=1
            ).astype(jnp.bfloat16)


def join_kernel(meta_ref, piece_ref, *refs):
    out_ref = refs[-1]
    width = piece_ref.shape[2]
    per = width // NS
    source = lax.broadcasted_iota(jnp.int32, (width, width), 0)
    target = lax.broadcasted_iota(jnp.int32, (width, width), 1)
    move = (target == (source % per) * NS + source // per).astype(jnp.float32)
    move = move.astype(jnp.bfloat16)
    for part in range(2):
        out_ref[0, part] = jnp.dot(
            piece_ref[part], move, preferred_element_type=jnp.float32
        ).astype(jnp.bfloat16)


def body(eigenvectors, gauge_links, momenta, displacement, slice_pairs, perambulators):
    bf16, f32, i32 = jnp.bfloat16, jnp.float32, jnp.int32
    fields = eigenvectors[0]
    links = gauge_links[0]
    planes, sites, vectors = fields.shape[2:]
    slab, tiles = lax.axis_size("slab"), lax.axis_size("tile")
    z, t, core = lax.axis_index("slab"), lax.axis_index("tile"), lax.axis_index("spin")
    z, t, core = z.astype(i32), t.astype(i32), core.astype(i32)
    lattice_x = planes * slab
    normalize = 1.0 / math.sqrt(3072 * lattice_x * LY * LZ)

    rim = shift(fields[:, :, 0], "slab", -1)

    elems = jnp.stack([core, 1 - core])
    forward = (displacement[elems] == 1).astype(i32)
    turns = momenta[elems]
    x_site = z * planes + jnp.arange(planes, dtype=i32)[None, :] + (1 - forward)[:, None]
    yz_site = core * sites + jnp.arange(sites, dtype=i32)
    wave_x = jnp.mod(turns[:, 0:1] * x_site, lattice_x)
    wave_y = jnp.mod(turns[:, 1:2] * (yz_site // LZ)[None, :], LY)
    wave_z = jnp.mod(turns[:, 2:3] * (yz_site % LZ)[None, :], LZ)
    number = (
        wave_x[:, :, None] * (LY * LZ)
        + (wave_y * (lattice_x * LZ) + wave_z * (lattice_x * LY))[:, None, :]
    )
    angle = number.astype(f32) * (2.0 * math.pi / (lattice_x * LY * LZ))
    sign = (2 * forward - 1).astype(f32)[:, None, None]
    turn = jnp.stack([jnp.cos(angle), jnp.sin(angle) * sign], axis=1)
    coefs = jnp.concatenate(
        [
            links.reshape(2 * COLORS * COLORS, planes, sites),
            turn.reshape(4, planes, sites),
            jnp.zeros((COEFS - 2 * COLORS * COLORS - 4, planes, sites), f32),
        ]
    ).transpose(1, 2, 0)

    block = min(sites, 256)
    inner, outer = pl.pallas_call(
        field_kernel,
        grid=(sites // block,),
        in_specs=[
            pl.BlockSpec((2, COLORS, planes, block, vectors), lambda i: (0, 0, 0, i, 0)),
            pl.BlockSpec((planes, block, COEFS), lambda i: (0, i, 0)),
        ],
        out_specs=[
            pl.BlockSpec((4 * vectors, 2 * vectors), lambda i: (0, 0)),
            pl.BlockSpec((COLORS, 4 * vectors, block), lambda i: (0, 0, i)),
        ],
        out_shape=[
            jax.ShapeDtypeStruct((4 * vectors, 2 * vectors), f32),
            jax.ShapeDtypeStruct((COLORS, 4 * vectors, sites), bf16),
        ],
        scratch_shapes=[pltpu.VMEM((COLORS, block, 4 * vectors), bf16)],
        name="fields",
    )(fields, coefs)

    parity = lax.rem(z, 2)
    pairs = perambulators.shape[0]
    spin_rows = perambulators.shape[2] // vectors
    width = perambulators.shape[3]
    items = pairs * spin_rows
    share = slab // items
    assert share * items == slab and (share * spin_rows) % 2 == 0
    chosen = slice_pairs[z // share // spin_rows]
    meta = jnp.stack([core, parity, chosen[0], chosen[1], z, displacement[0], displacement[1]])

    keep, send = pl.pallas_call(
        functools.partial(rim_kernel, normalize),
        in_specs=[smem()] + [vmem()] * 3,
        out_specs=[vmem()] * 2,
        out_shape=[
            jax.ShapeDtypeStruct((2, vectors, vectors), f32),
            jax.ShapeDtypeStruct((2, vectors, vectors), bf16),
        ],
        name="rim",
    )(meta, outer, inner, rim)

    with jax.named_scope("halves"):
        half = keep + swap(send, "spin", 1).astype(f32)
    with jax.named_scope("quarters"):
        quarter = half[0] + swap(half[1].astype(bf16), "slab", 1).astype(f32)
    distance = 2
    while distance < slab:
        with jax.named_scope(f"sum{distance}"):
            quarter = quarter + swap(quarter.astype(bf16), "slab", distance).astype(f32)
        distance *= 2
    quarter = quarter.astype(bf16)
    wanted = lax.rem(t - chosen[core] + tiles, tiles)
    own = quarter
    for by in range(1, tiles):
        with jax.named_scope(f"tile{by}"):
            own = jnp.where(wanted == by, shift(quarter, "tile", by), own)
    with jax.named_scope("pair"):
        pair = swap(own, "slab", 1)
    with jax.named_scope("own_core"):
        own_core = swap(own, "spin", 1)
    with jax.named_scope("pair_core"):
        pair_core = swap(pair, "spin", 1)

    blocks = pl.pallas_call(
        functools.partial(deal_kernel, share),
        in_specs=[smem(), vmem()],
        out_specs=[vmem()] * slab,
        out_shape=[jax.ShapeDtypeStruct((2, vectors, width), bf16)] * slab,
        name="deal",
    )(meta, perambulators.reshape(pairs, 2, spin_rows, vectors, width))
    chunks = [blocks[0]]
    for by in range(1, slab):
        with jax.named_scope(f"deal{by}"):
            value = lax.optimization_barrier((rim, blocks[by]))[1]
            chunks.append(swap(value, "slab", by))

    count = slab // share
    pieces = pl.pallas_call(
        functools.partial(block_kernel, slab, share),
        in_specs=[smem()] + [vmem()] * (4 + slab),
        out_specs=[vmem()] * count,
        out_shape=[jax.ShapeDtypeStruct((2, vectors, width), bf16)] * count,
        scratch_shapes=[
            pltpu.VMEM((vectors, vectors), f32),
            pltpu.VMEM((vectors, 2 * vectors // share), f32),
        ],
        name="blocks",
    )(meta, own, pair, own_core, pair_core, *chunks)

    result = None
    for which, piece in enumerate(pieces):
        route = [
            (s, (s % share) * count + ((s // share) ^ which)) for s in range(slab)
        ]
        if any(a != b for a, b in route):
            with jax.named_scope(f"out{which}"):
                piece = lax.ppermute(piece, "slab", route)
        item = lax.rem(z, count) ^ which
        place = jnp.stack([item // spin_rows, lax.rem(item, spin_rows)])
        out_spec = pl.BlockSpec(
            (1, 2, vectors, width), lambda i, at: (at[0], 0, at[1], 0)
        )
        previous = [] if result is None else [result]
        result = pl.pallas_call(
            join_kernel,
            grid_spec=pltpu.PrefetchScalarGridSpec(
                num_scalar_prefetch=1,
                grid=(1,),
                in_specs=[pl.BlockSpec((2, vectors, width), lambda i, at: (0, 0, 0))]
                + [pl.BlockSpec(memory_space=pl.ANY)] * len(previous),
                out_specs=out_spec,
            ),
            out_shape=jax.ShapeDtypeStruct(perambulators.shape, bf16),
            input_output_aliases={2: 0} if previous else {},
            name="join",
        )(place, piece, *previous)
    return result


def solution(mesh):
    return jax.shard_map(
        body,
        mesh=mesh,
        in_specs=(
            P(("cfg", "tile"), None, None, "slab", "spin", None),
            P(("cfg", "tile"), None, None, None, "slab", "spin"),
            P(),
            P(),
            P("tile", None),
            P(("cfg", "tile"), None, "spin", "slab"),
        ),
        out_specs=P(("cfg", "tile"), None, "spin", "slab"),
        check_vma=False,
    )
```

```python
import functools
import math

import jax
import jax.numpy as jnp
from jax import lax
from jax.experimental import pallas as pl
from jax.experimental.pallas import tpu as pltpu
from jax.sharding import PartitionSpec as P


NS = 4
LY = 32
LZ = 32
COLORS = 3
COEFS = 24


def shift(x, axis, by):
    count = lax.axis_size(axis)
    return lax.ppermute(x, axis, [(i, (i + by) % count) for i in range(count)])


def swap(x, axis, distance):
    count = lax.axis_size(axis)
    return lax.ppermute(x, axis, [(i, i ^ distance) for i in range(count)])


def vmem():
    return pl.BlockSpec(memory_space=pltpu.VMEM)


def smem():
    return pl.BlockSpec(memory_space=pltpu.SMEM)


def edge_kernel(fields_ref, edge_ref, held, taken, given):
    spots = [(part, c) for part in range(2) for c in range(COLORS)]

    def take(at, spot):
        return pltpu.make_async_copy(
            fields_ref.at[spot[0], spot[1], 0], held.at[at], taken.at[at]
        )

    def give(at, spot):
        return pltpu.make_async_copy(held.at[at], edge_ref.at[spot[0], spot[1]], given.at[at])

    for at, spot in enumerate(spots):
        take(at, spot).start()
    for at, spot in enumerate(spots):
        take(at, spot).wait()
        give(at, spot).start()
    for at, spot in enumerate(spots):
        give(at, spot).wait()


def field_kernel(meta_ref, fields_ref, coefs_ref, inner_ref, outer_ref, rotated):
    planes, block, vectors = fields_ref.shape[2:]
    tile = 16

    @pl.when(pl.program_id(0) == 0)
    def _():
        inner_ref[...] = jnp.zeros_like(inner_ref)

    for plane in range(planes):

        def rows_step(step, carry):
            rows = pl.ds(pl.multiple_of(step * tile, tile), tile)
            coefs = coefs_ref[plane, rows, :]

            def coef(which):
                return coefs[:, which : which + 1]

            real = [fields_ref[0, c, plane, rows, :].astype(jnp.float32) for c in range(COLORS)]
            imag = [fields_ref[1, c, plane, rows, :].astype(jnp.float32) for c in range(COLORS)]
            for out in range(COLORS):
                local_real = None
                for c in range(COLORS):
                    link_real = coef(COLORS * c + out)
                    link_imag = coef(COLORS * COLORS + COLORS * c + out)
                    term_real = link_real * real[c] + link_imag * imag[c]
                    term_imag = link_real * imag[c] - link_imag * real[c]
                    local_real = term_real if local_real is None else local_real + term_real
                    local_imag = term_imag if c == 0 else local_imag + term_imag
                for slot in range(2):
                    turn_real = coef(2 * COLORS * COLORS + 2 * slot)
                    turn_imag = coef(2 * COLORS * COLORS + 2 * slot + 1)
                    at = 2 * slot * vectors
                    rotated[out, rows, at : at + vectors] = (
                        turn_real * local_real - turn_imag * local_imag
                    ).astype(jnp.bfloat16)
                    at += vectors
                    rotated[out, rows, at : at + vectors] = (
                        turn_real * local_imag + turn_imag * local_real
                    ).astype(jnp.bfloat16)
            return carry

        lax.fori_loop(0, block // tile, rows_step, 0)
        for c in range(COLORS):
            if plane + 1 < planes:
                ahead = jnp.concatenate(
                    [fields_ref[0, c, plane + 1], fields_ref[1, c, plane + 1]], axis=1
                )
                inner_ref[...] += lax.dot_general(
                    rotated[c], ahead, (((0,), (0,)), ((), ())), preferred_element_type=jnp.float32
                )
            else:
                outer_ref[c] = rotated[c].T


def rim_kernel(normalize, meta_ref, outer_ref, inner_ref, rim_ref, keep_ref, send_ref):
    vectors = rim_ref.shape[-1]
    for slot, out in ((1, send_ref), (0, keep_ref)):
        at = 2 * slot * vectors
        totals = []
        for part in range(2):
            total = inner_ref[at : at + 2 * vectors, part * vectors : (part + 1) * vectors]
            for c in range(COLORS):
                total = total + jnp.dot(
                    outer_ref[c, at : at + 2 * vectors, :],
                    rim_ref[part, c],
                    preferred_element_type=jnp.float32,
                )
            totals.append(total)
        real = totals[0][:vectors] + totals[1][vectors:]
        imag = totals[0][vectors:] - totals[1][:vectors]
        out[meta_ref[1]] = (real * normalize).astype(out.dtype)
        out[1 - meta_ref[1]] = (imag * normalize).astype(out.dtype)


def deal_kernel(share, meta_ref, perams_ref, move_ref, *outs):
    spin_rows = perams_ref.shape[2]
    for by, out in enumerate(outs):
        item = (meta_ref[4] ^ by) // share
        for part in range(2):
            out[part] = jnp.dot(
                perams_ref[item // spin_rows, part, lax.rem(item, spin_rows)],
                move_ref[...],
                preferred_element_type=jnp.float32,
            ).astype(jnp.bfloat16)


def block_kernel(slab, share, meta_ref, *refs):
    parts = refs[:4]
    chunks = refs[4 : 4 + slab]
    outs = refs[4 + slab : -2]
    table_ref, turned_ref = refs[-2:]
    vectors = parts[0].shape[0]
    per = vectors // slab
    core, parity, place = meta_ref[0], meta_ref[1], meta_ref[4]
    found = [piece[...].astype(jnp.float32) for piece in parts]

    def pick(elem):
        mine = core == elem
        first = jnp.where(mine, found[0], found[2])
        second = jnp.where(mine, found[1], found[3])
        real = jnp.where(parity == 0, first, second)
        imag = jnp.where(parity == 0, second, first)
        forward = meta_ref[5 + elem] == 1
        return (
            jnp.where(forward, real, real.T),
            jnp.where(forward, -imag, imag.T),
        )

    real, imag = pick(0)
    real, imag = real.astype(jnp.bfloat16), imag.astype(jnp.bfloat16)
    matrix = jnp.concatenate(
        [jnp.concatenate([real, -imag], axis=1), jnp.concatenate([imag, real], axis=1)], axis=0
    )
    columns = []
    for spin in range(NS):
        at = spin * per
        columns += [
            chunk[...].reshape(2 * vectors, NS * per)[:, at : at + per] for chunk in chunks
        ]
    spread = jnp.concatenate(columns, axis=1)
    left = jnp.dot(matrix, spread, preferred_element_type=jnp.float32).astype(jnp.bfloat16)
    width = vectors // share
    count = slab // share
    lane = lax.broadcasted_iota(jnp.int32, (per, width), 1) // per
    for part, value in enumerate(pick(1)):
        table_ref[...] = value
        for chunk in range(slab):
            row = pl.multiple_of((place ^ chunk) * per, per)
            rows = table_ref[pl.ds(row, per), :]
            turned = rows[:, :width]
            for group in range(1, share):
                turned = jnp.where(
                    lax.rem(place, share) == group,
                    rows[:, group * width : (group + 1) * width],
                    turned,
                )
            step = 1
            while step < count:
                down = pltpu.roll(turned, step * per, 1)
                up = pltpu.roll(turned, width - step * per, 1)
                moved = jnp.where((lane // step) % 2 == 0, up, down)
                turned = jnp.where((place // (share * step)) % 2 == 1, moved, turned)
                step *= 2
            turned_ref[chunk * per : (chunk + 1) * per, part * width : (part + 1) * width] = (
                turned
            )
    right = turned_ref[...].astype(jnp.bfloat16)
    reals, imags = [], []
    for spin in range(NS):
        both = jnp.dot(
            left[:, spin * vectors : (spin + 1) * vectors],
            right,
            preferred_element_type=jnp.float32,
        )
        reals.append(both[:vectors, :width] - both[vectors:, width:])
        imags.append(both[:vectors, width:] + both[vectors:, :width])
    for which, out in enumerate(outs):
        at = which * per
        for part, values in ((0, reals), (1, imags)):
            out[part] = jnp.concatenate(
                [value[:, at : at + per] for value in values], axis=1
            ).astype(jnp.bfloat16)


def join_kernel(count, place_ref, move_ref, *refs):
    out_ref = refs[-1]
    for which in range(count):

        @pl.when(pl.program_id(0) == which)
        def _():
            for part in range(2):
                out_ref[0, part] = jnp.dot(
                    refs[which][part], move_ref[...], preferred_element_type=jnp.float32
                ).astype(jnp.bfloat16)


def body(eigenvectors, gauge_links, momenta, displacement, slice_pairs, perambulators):
    bf16, f32, i32 = jnp.bfloat16, jnp.float32, jnp.int32
    fields = eigenvectors[0]
    links = gauge_links[0]
    planes, sites, vectors = fields.shape[2:]
    slab, tiles = lax.axis_size("slab"), lax.axis_size("tile")
    z, t, core = lax.axis_index("slab"), lax.axis_index("tile"), lax.axis_index("spin")
    z, t, core = z.astype(i32), t.astype(i32), core.astype(i32)
    lattice_x = planes * slab
    normalize = 1.0 / math.sqrt(3072 * lattice_x * LY * LZ)

    edge = pl.pallas_call(
        edge_kernel,
        in_specs=[pl.BlockSpec(memory_space=pl.ANY)],
        out_specs=pl.BlockSpec(memory_space=pl.ANY),
        out_shape=jax.ShapeDtypeStruct((2, COLORS, sites, vectors), bf16),
        scratch_shapes=[
            pltpu.VMEM((2 * COLORS, sites, vectors), bf16),
            pltpu.SemaphoreType.DMA((2 * COLORS,)),
            pltpu.SemaphoreType.DMA((2 * COLORS,)),
        ],
        compiler_params=pltpu.CompilerParams(vmem_limit_bytes=60 << 20),
        name="edge",
    )(fields)
    rim = shift(edge, "slab", -1)

    elems = jnp.stack([core, 1 - core])
    forward = (displacement[elems] == 1).astype(i32)
    turns = momenta[elems]
    x_site = z * planes + jnp.arange(planes, dtype=i32)[None, :] + (1 - forward)[:, None]
    yz_site = core * sites + jnp.arange(sites, dtype=i32)
    wave_x = jnp.mod(turns[:, 0:1] * x_site, lattice_x)
    wave_y = jnp.mod(turns[:, 1:2] * (yz_site // LZ)[None, :], LY)
    wave_z = jnp.mod(turns[:, 2:3] * (yz_site % LZ)[None, :], LZ)
    number = (
        wave_x[:, :, None] * (LY * LZ)
        + (wave_y * (lattice_x * LZ) + wave_z * (lattice_x * LY))[:, None, :]
    )
    angle = number.astype(f32) * (2.0 * math.pi / (lattice_x * LY * LZ))
    sign = (2 * forward - 1).astype(f32)[:, None, None]
    turn = jnp.stack([jnp.cos(angle), jnp.sin(angle) * sign], axis=1)
    coefs = jnp.concatenate(
        [
            links.reshape(2 * COLORS * COLORS, planes, sites),
            turn.reshape(4, planes, sites),
            jnp.zeros((COEFS - 2 * COLORS * COLORS - 4, planes, sites), f32),
        ]
    ).transpose(1, 2, 0)

    parity = lax.rem(z, 2)
    pairs = perambulators.shape[0]
    spin_rows = perambulators.shape[2] // vectors
    width = perambulators.shape[3]
    items = pairs * spin_rows
    share = slab // items
    assert share * items == slab and (share * spin_rows) % 2 == 0
    chosen = slice_pairs[z // share // spin_rows]
    meta = jnp.stack([core, parity, chosen[0], chosen[1], z, displacement[0], displacement[1]])

    per = width // NS
    column = jnp.arange(width, dtype=i32)
    target = (column % NS) * per + column // NS
    gather_spins = (target[:, None] == column[None, :]).astype(bf16)
    spread_spins = (target[None, :] == column[:, None]).astype(bf16)
    count = slab // share

    def places(first, last):
        found = lax.rem(z, count) ^ jnp.arange(first, last, dtype=i32)
        return jnp.concatenate([found // spin_rows, lax.rem(found, spin_rows)])

    cuts = (0, count // 2, count)
    wanted = lax.rem(t - chosen[core] + tiles, tiles)
    spots = [places(first, last) for first, last in zip(cuts[:-1], cuts[1:])]
    meta, coefs, gather_spins, spread_spins, wanted, spots = lax.optimization_barrier(
        (meta, coefs, gather_spins, spread_spins, wanted, spots)
    )

    block = min(sites, 256)
    inner, outer = pl.pallas_call(
        field_kernel,
        grid=(sites // block,),
        in_specs=[
            smem(),
            pl.BlockSpec((2, COLORS, planes, block, vectors), lambda i: (0, 0, 0, i, 0)),
            pl.BlockSpec((planes, block, COEFS), lambda i: (0, i, 0)),
        ],
        out_specs=[
            pl.BlockSpec((4 * vectors, 2 * vectors), lambda i: (0, 0)),
            pl.BlockSpec((COLORS, 4 * vectors, block), lambda i: (0, 0, i)),
        ],
        out_shape=[
            jax.ShapeDtypeStruct((4 * vectors, 2 * vectors), f32),
            jax.ShapeDtypeStruct((COLORS, 4 * vectors, sites), bf16),
        ],
        scratch_shapes=[pltpu.VMEM((COLORS, block, 4 * vectors), bf16)],
        compiler_params=pltpu.CompilerParams(vmem_limit_bytes=15 << 20),
        name="fields",
    )(meta, fields, coefs)

    blocks = pl.pallas_call(
        functools.partial(deal_kernel, share),
        in_specs=[smem(), vmem(), vmem()],
        out_specs=[vmem()] * slab,
        out_shape=[jax.ShapeDtypeStruct((2, vectors, width), bf16)] * slab,
        compiler_params=pltpu.CompilerParams(vmem_limit_bytes=8 << 20),
        name="deal",
    )(meta, perambulators.reshape(pairs, 2, spin_rows, vectors, width), gather_spins)
    outer, *blocks = lax.optimization_barrier((outer, *blocks))

    keep, send = pl.pallas_call(
        functools.partial(rim_kernel, normalize),
        in_specs=[smem()] + [vmem()] * 3,
        out_specs=[vmem()] * 2,
        out_shape=[
            jax.ShapeDtypeStruct((2, vectors, vectors), f32),
            jax.ShapeDtypeStruct((2, vectors, vectors), bf16),
        ],
        compiler_params=pltpu.CompilerParams(vmem_limit_bytes=14 << 20),
        name="rim",
    )(meta, outer, inner, rim)

    half = keep + swap(send, "spin", 1).astype(f32)
    quarter = half[0] + swap(half[1].astype(bf16), "slab", 1).astype(f32)
    distance = 2
    while distance < slab:
        quarter = quarter + swap(quarter.astype(bf16), "slab", distance).astype(f32)
        distance *= 2
    quarter = quarter.astype(bf16)
    own = quarter
    for by in range(1, tiles):
        own = jnp.where(wanted == by, shift(quarter, "tile", by), own)
    pair = swap(own, "slab", 1)
    own_core = swap(own, "spin", 1)
    pair_core = swap(pair, "spin", 1)

    chunks = [blocks[0]]
    for by in range(1, slab):
        chunks.append(swap(blocks[by], "slab", by))

    pieces = pl.pallas_call(
        functools.partial(block_kernel, slab, share),
        in_specs=[smem()] + [vmem()] * (4 + slab),
        out_specs=[vmem()] * count,
        out_shape=[jax.ShapeDtypeStruct((2, vectors, width), bf16)] * count,
        scratch_shapes=[
            pltpu.VMEM((vectors, vectors), f32),
            pltpu.VMEM((vectors, 2 * vectors // share), f32),
        ],
        compiler_params=pltpu.CompilerParams(vmem_limit_bytes=14 << 20),
        name="blocks",
    )(meta, own, pair, own_core, pair_core, *chunks)

    arrived = []
    for which, piece in enumerate(pieces):
        route = [(s, (s % share) * count + ((s // share) ^ which)) for s in range(slab)]
        if any(a != b for a, b in route):
            piece = lax.ppermute(piece, "slab", route)
        arrived.append(piece)

    result = []
    for first, last, spot in zip(cuts[:-1], cuts[1:], spots):
        span = last - first
        result = [
            pl.pallas_call(
                functools.partial(join_kernel, span),
                grid_spec=pltpu.PrefetchScalarGridSpec(
                    num_scalar_prefetch=1,
                    grid=(span,),
                    in_specs=[vmem()] * (1 + span)
                    + [pl.BlockSpec(memory_space=pl.ANY)] * len(result),
                    out_specs=pl.BlockSpec(
                        (1, 2, vectors, width),
                        lambda i, at, span=span: (at[i], 0, at[span + i], 0),
                    ),
                ),
                out_shape=jax.ShapeDtypeStruct(perambulators.shape, bf16),
                input_output_aliases={2 + span: 0} if result else {},
                compiler_params=pltpu.CompilerParams(vmem_limit_bytes=6 << 20),
                name="join",
            )(spot, spread_spins, *arrived[first:last], *result)
        ]
    return result[0]


def solution(mesh):
    return jax.shard_map(
        body,
        mesh=mesh,
        in_specs=(
            P(("cfg", "tile"), None, None, "slab", "spin", None),
            P(("cfg", "tile"), None, None, None, "slab", "spin"),
            P(),
            P(),
            P("tile", None),
            P(("cfg", "tile"), None, "spin", "slab"),
        ),
        out_specs=P(("cfg", "tile"), None, "spin", "slab"),
        check_vma=False,
    )
```

```python
import functools
import math

import jax
import jax.numpy as jnp
from jax import lax
from jax.experimental import pallas as pl
from jax.experimental.pallas import tpu as pltpu
from jax.sharding import PartitionSpec as P


NS = 4
LY = 32
LZ = 32
COLORS = 3
COEFS = 24


def shift(x, axis, by):
    count = lax.axis_size(axis)
    return lax.ppermute(x, axis, [(i, (i + by) % count) for i in range(count)])


def swap(x, axis, distance):
    count = lax.axis_size(axis)
    return lax.ppermute(x, axis, [(i, i ^ distance) for i in range(count)])


def vmem():
    return pl.BlockSpec(memory_space=pltpu.VMEM)


def smem():
    return pl.BlockSpec(memory_space=pltpu.SMEM)


def edge_kernel(fields_ref, most_ref, last_ref, taken):
    spots = [(part, c) for part in range(2) for c in range(COLORS)]
    copies = [
        pltpu.make_async_copy(
            fields_ref.at[part, c, 0],
            most_ref.at[at] if at + 1 < len(spots) else last_ref,
            taken.at[at],
        )
        for at, (part, c) in enumerate(spots)
    ]
    for copy in copies:
        copy.start()
    for copy in copies:
        copy.wait()


def field_kernel(meta_ref, fields_ref, coefs_ref, inner_ref, outer_ref, rotated):
    planes, block, vectors = fields_ref.shape[2:]
    tile = 16

    @pl.when(pl.program_id(0) == 0)
    def _():
        inner_ref[...] = jnp.zeros_like(inner_ref)

    for plane in range(planes):

        def rows_step(step, carry):
            rows = pl.ds(pl.multiple_of(step * tile, tile), tile)
            coefs = coefs_ref[plane, rows, :]

            def coef(which):
                return coefs[:, which : which + 1]

            real = [fields_ref[0, c, plane, rows, :].astype(jnp.float32) for c in range(COLORS)]
            imag = [fields_ref[1, c, plane, rows, :].astype(jnp.float32) for c in range(COLORS)]
            for out in range(COLORS):
                local_real = None
                for c in range(COLORS):
                    link_real = coef(COLORS * c + out)
                    link_imag = coef(COLORS * COLORS + COLORS * c + out)
                    term_real = link_real * real[c] + link_imag * imag[c]
                    term_imag = link_real * imag[c] - link_imag * real[c]
                    local_real = term_real if local_real is None else local_real + term_real
                    local_imag = term_imag if c == 0 else local_imag + term_imag
                for slot in range(2):
                    turn_real = coef(2 * COLORS * COLORS + 2 * slot)
                    turn_imag = coef(2 * COLORS * COLORS + 2 * slot + 1)
                    at = 2 * slot * vectors
                    rotated[out, rows, at : at + vectors] = (
                        turn_real * local_real - turn_imag * local_imag
                    ).astype(jnp.bfloat16)
                    at += vectors
                    rotated[out, rows, at : at + vectors] = (
                        turn_real * local_imag + turn_imag * local_real
                    ).astype(jnp.bfloat16)
            return carry

        lax.fori_loop(0, block // tile, rows_step, 0)
        for c in range(COLORS):
            if plane + 1 < planes:
                ahead = jnp.concatenate(
                    [fields_ref[0, c, plane + 1], fields_ref[1, c, plane + 1]], axis=1
                )
                inner_ref[...] += lax.dot_general(
                    rotated[c], ahead, (((0,), (0,)), ((), ())), preferred_element_type=jnp.float32
                )
            else:
                outer_ref[c] = rotated[c].T


def most_kernel(outer_ref, inner_ref, most_ref, total_ref):
    vectors = most_ref.shape[-1]
    for slot in range(2):
        at = 2 * slot * vectors
        totals = []
        for part in range(2):
            total = inner_ref[at : at + 2 * vectors, part * vectors : (part + 1) * vectors]
            for c in range(COLORS - part):
                total = total + jnp.dot(
                    outer_ref[c, at : at + 2 * vectors, :],
                    most_ref[COLORS * part + c],
                    preferred_element_type=jnp.float32,
                )
            totals.append(total)
        total_ref[slot, 0] = totals[0][:vectors] + totals[1][vectors:]
        total_ref[slot, 1] = totals[0][vectors:] - totals[1][:vectors]


def last_kernel(normalize, meta_ref, outer_ref, total_ref, last_ref, keep_ref, send_ref):
    vectors = last_ref.shape[-1]
    for slot, out in ((1, send_ref), (0, keep_ref)):
        at = 2 * slot * vectors
        both = jnp.dot(
            outer_ref[0, at : at + 2 * vectors, :],
            last_ref[...],
            preferred_element_type=jnp.float32,
        )
        real = total_ref[slot, 0] + both[vectors:]
        imag = total_ref[slot, 1] - both[:vectors]
        out[meta_ref[1]] = (real * normalize).astype(out.dtype)
        out[1 - meta_ref[1]] = (imag * normalize).astype(out.dtype)


def deal_kernel(share, meta_ref, perams_ref, move_ref, *outs):
    spin_rows = perams_ref.shape[2]
    for by, out in enumerate(outs):
        item = (meta_ref[4] ^ by) // share
        for part in range(2):
            out[part] = jnp.dot(
                perams_ref[item // spin_rows, part, lax.rem(item, spin_rows)],
                move_ref[...],
                preferred_element_type=jnp.float32,
            ).astype(jnp.bfloat16)


def block_kernel(slab, share, meta_ref, *refs):
    parts = refs[:4]
    chunks = refs[4 : 4 + slab]
    outs = refs[4 + slab : -2]
    table_ref, turned_ref = refs[-2:]
    vectors = parts[0].shape[0]
    per = vectors // slab
    core, parity, place = meta_ref[0], meta_ref[1], meta_ref[4]
    found = [piece[...].astype(jnp.float32) for piece in parts]

    def pick(elem):
        mine = core == elem
        first = jnp.where(mine, found[0], found[2])
        second = jnp.where(mine, found[1], found[3])
        real = jnp.where(parity == 0, first, second)
        imag = jnp.where(parity == 0, second, first)
        forward = meta_ref[5 + elem] == 1
        return (
            jnp.where(forward, real, real.T),
            jnp.where(forward, -imag, imag.T),
        )

    real, imag = pick(0)
    real, imag = real.astype(jnp.bfloat16), imag.astype(jnp.bfloat16)
    matrix = jnp.concatenate(
        [jnp.concatenate([real, -imag], axis=1), jnp.concatenate([imag, real], axis=1)], axis=0
    )
    columns = []
    for spin in range(NS):
        at = spin * per
        columns += [
            chunk[...].reshape(2 * vectors, NS * per)[:, at : at + per] for chunk in chunks
        ]
    spread = jnp.concatenate(columns, axis=1)
    left = jnp.dot(matrix, spread, preferred_element_type=jnp.float32).astype(jnp.bfloat16)
    width = vectors // share
    count = slab // share
    lane = lax.broadcasted_iota(jnp.int32, (per, width), 1) // per
    for part, value in enumerate(pick(1)):
        table_ref[...] = value
        for chunk in range(slab):
            row = pl.multiple_of((place ^ chunk) * per, per)
            rows = table_ref[pl.ds(row, per), :]
            turned = rows[:, :width]
            for group in range(1, share):
                turned = jnp.where(
                    lax.rem(place, share) == group,
                    rows[:, group * width : (group + 1) * width],
                    turned,
                )
            step = 1
            while step < count:
                down = pltpu.roll(turned, step * per, 1)
                up = pltpu.roll(turned, width - step * per, 1)
                moved = jnp.where((lane // step) % 2 == 0, up, down)
                turned = jnp.where((place // (share * step)) % 2 == 1, moved, turned)
                step *= 2
            turned_ref[chunk * per : (chunk + 1) * per, part * width : (part + 1) * width] = (
                turned
            )
    right = turned_ref[...].astype(jnp.bfloat16)
    reals, imags = [], []
    for spin in range(NS):
        both = jnp.dot(
            left[:, spin * vectors : (spin + 1) * vectors],
            right,
            preferred_element_type=jnp.float32,
        )
        reals.append(both[:vectors, :width] - both[vectors:, width:])
        imags.append(both[:vectors, width:] + both[vectors:, :width])
    for which, out in enumerate(outs):
        at = which * per
        for part, values in ((0, reals), (1, imags)):
            out[part] = jnp.concatenate(
                [value[:, at : at + per] for value in values], axis=1
            ).astype(jnp.bfloat16)


def join_kernel(count, place_ref, move_ref, *refs):
    out_ref = refs[-1]
    for which in range(count):

        @pl.when(pl.program_id(0) == which)
        def _():
            for part in range(2):
                out_ref[0, part] = jnp.dot(
                    refs[which][part], move_ref[...], preferred_element_type=jnp.float32
                ).astype(jnp.bfloat16)


def body(eigenvectors, gauge_links, momenta, displacement, slice_pairs, perambulators):
    bf16, f32, i32 = jnp.bfloat16, jnp.float32, jnp.int32
    fields = eigenvectors[0]
    links = gauge_links[0]
    planes, sites, vectors = fields.shape[2:]
    slab, tiles = lax.axis_size("slab"), lax.axis_size("tile")
    z, t, core = lax.axis_index("slab"), lax.axis_index("tile"), lax.axis_index("spin")
    z, t, core = z.astype(i32), t.astype(i32), core.astype(i32)
    lattice_x = planes * slab
    normalize = 1.0 / math.sqrt(3072 * lattice_x * LY * LZ)

    most, last = pl.pallas_call(
        edge_kernel,
        in_specs=[pl.BlockSpec(memory_space=pl.ANY)],
        out_specs=[vmem()] * 2,
        out_shape=[
            jax.ShapeDtypeStruct((2 * COLORS - 1, sites, vectors), bf16),
            jax.ShapeDtypeStruct((sites, vectors), bf16),
        ],
        scratch_shapes=[pltpu.SemaphoreType.DMA((2 * COLORS,))],
        compiler_params=pltpu.CompilerParams(vmem_limit_bytes=62 << 20),
        name="edge",
    )(fields)
    most = shift(most, "slab", -1)
    last = shift(last, "slab", -1)

    elems = jnp.stack([core, 1 - core])
    forward = (displacement[elems] == 1).astype(i32)
    turns = momenta[elems]
    x_site = z * planes + jnp.arange(planes, dtype=i32)[None, :] + (1 - forward)[:, None]
    yz_site = core * sites + jnp.arange(sites, dtype=i32)
    wave_x = jnp.mod(turns[:, 0:1] * x_site, lattice_x)
    wave_y = jnp.mod(turns[:, 1:2] * (yz_site // LZ)[None, :], LY)
    wave_z = jnp.mod(turns[:, 2:3] * (yz_site % LZ)[None, :], LZ)
    number = (
        wave_x[:, :, None] * (LY * LZ)
        + (wave_y * (lattice_x * LZ) + wave_z * (lattice_x * LY))[:, None, :]
    )
    angle = number.astype(f32) * (2.0 * math.pi / (lattice_x * LY * LZ))
    sign = (2 * forward - 1).astype(f32)[:, None, None]
    turn = jnp.stack([jnp.cos(angle), jnp.sin(angle) * sign], axis=1)
    coefs = jnp.concatenate(
        [
            links.reshape(2 * COLORS * COLORS, planes, sites),
            turn.reshape(4, planes, sites),
            jnp.zeros((COEFS - 2 * COLORS * COLORS - 4, planes, sites), f32),
        ]
    ).transpose(1, 2, 0)

    parity = lax.rem(z, 2)
    pairs = perambulators.shape[0]
    spin_rows = perambulators.shape[2] // vectors
    width = perambulators.shape[3]
    items = pairs * spin_rows
    share = slab // items
    assert share * items == slab and (share * spin_rows) % 2 == 0
    chosen = slice_pairs[z // share // spin_rows]
    meta = jnp.stack([core, parity, chosen[0], chosen[1], z, displacement[0], displacement[1]])

    per = width // NS
    column = jnp.arange(width, dtype=i32)
    target = (column % NS) * per + column // NS
    gather_spins = (target[:, None] == column[None, :]).astype(bf16)
    spread_spins = (target[None, :] == column[:, None]).astype(bf16)
    count = slab // share

    def places(first, last):
        found = lax.rem(z, count) ^ jnp.arange(first, last, dtype=i32)
        return jnp.concatenate([found // spin_rows, lax.rem(found, spin_rows)])

    cuts = (0, count // 2, count)
    wanted = [
        lax.rem(t - slice_pairs[place // share // spin_rows, core] + tiles, tiles)
        for place in (z, z ^ 2)
    ]
    spots = [places(first, last) for first, last in zip(cuts[:-1], cuts[1:])]
    meta, coefs, gather_spins, spread_spins, wanted, spots = lax.optimization_barrier(
        (meta, coefs, gather_spins, spread_spins, wanted, spots)
    )

    block = min(sites, 256)
    inner, outer = pl.pallas_call(
        field_kernel,
        grid=(sites // block,),
        in_specs=[
            smem(),
            pl.BlockSpec((2, COLORS, planes, block, vectors), lambda i: (0, 0, 0, i, 0)),
            pl.BlockSpec((planes, block, COEFS), lambda i: (0, i, 0)),
        ],
        out_specs=[
            pl.BlockSpec((4 * vectors, 2 * vectors), lambda i: (0, 0)),
            pl.BlockSpec((COLORS, 4 * vectors, block), lambda i: (0, 0, i)),
        ],
        out_shape=[
            jax.ShapeDtypeStruct((4 * vectors, 2 * vectors), f32),
            jax.ShapeDtypeStruct((COLORS, 4 * vectors, sites), bf16),
        ],
        scratch_shapes=[pltpu.VMEM((COLORS, block, 4 * vectors), bf16)],
        compiler_params=pltpu.CompilerParams(vmem_limit_bytes=15 << 20),
        name="fields",
    )(meta, fields, coefs)

    blocks = pl.pallas_call(
        functools.partial(deal_kernel, share),
        in_specs=[smem(), vmem(), vmem()],
        out_specs=[vmem()] * slab,
        out_shape=[jax.ShapeDtypeStruct((2, vectors, width), bf16)] * slab,
        compiler_params=pltpu.CompilerParams(vmem_limit_bytes=8 << 20),
        name="deal",
    )(meta, perambulators.reshape(pairs, 2, spin_rows, vectors, width), gather_spins)
    outer, *blocks = lax.optimization_barrier((outer, *blocks))

    total = pl.pallas_call(
        most_kernel,
        in_specs=[vmem()] * 3,
        out_specs=vmem(),
        out_shape=jax.ShapeDtypeStruct((2, 2, vectors, vectors), f32),
        compiler_params=pltpu.CompilerParams(vmem_limit_bytes=14 << 20),
        name="most",
    )(outer, inner, most)
    keep, send = pl.pallas_call(
        functools.partial(last_kernel, normalize),
        grid=(1,),
        in_specs=[
            smem(),
            pl.BlockSpec((1, 4 * vectors, sites), lambda i: (COLORS - 1, 0, 0)),
            vmem(),
            vmem(),
        ],
        out_specs=[vmem()] * 2,
        out_shape=[
            jax.ShapeDtypeStruct((2, vectors, vectors), f32),
            jax.ShapeDtypeStruct((2, vectors, vectors), bf16),
        ],
        compiler_params=pltpu.CompilerParams(vmem_limit_bytes=10 << 20),
        name="last",
    )(meta, outer, total, last)

    half = keep + swap(send, "spin", 1).astype(f32)
    quarter = half[0] + swap(half[1].astype(bf16), "slab", 1).astype(f32)
    distance = 4
    while distance < slab:
        quarter = quarter + swap(quarter.astype(bf16), "slab", distance).astype(f32)
        distance *= 2
    own, theirs = quarter, quarter.astype(bf16)
    for by in range(1, tiles):
        moved = shift(quarter.astype(bf16), "tile", by)
        own = jnp.where(wanted[0] == by, moved.astype(f32), own)
        theirs = jnp.where(wanted[1] == by, moved, theirs)
    own = (own + swap(theirs, "slab", 2).astype(f32)).astype(bf16)
    pair = swap(own, "slab", 1)
    own_core = swap(own, "spin", 1)
    pair_core = swap(pair, "spin", 1)

    chunks = [blocks[0]]
    for by in range(1, slab):
        chunks.append(swap(blocks[by], "slab", by))

    pieces = pl.pallas_call(
        functools.partial(block_kernel, slab, share),
        in_specs=[smem()] + [vmem()] * (4 + slab),
        out_specs=[vmem()] * count,
        out_shape=[jax.ShapeDtypeStruct((2, vectors, width), bf16)] * count,
        scratch_shapes=[
            pltpu.VMEM((vectors, vectors), f32),
            pltpu.VMEM((vectors, 2 * vectors // share), f32),
        ],
        compiler_params=pltpu.CompilerParams(vmem_limit_bytes=14 << 20),
        name="blocks",
    )(meta, own, pair, own_core, pair_core, *chunks)

    arrived = []
    for which, piece in enumerate(pieces):
        route = [(s, (s % share) * count + ((s // share) ^ which)) for s in range(slab)]
        if any(a != b for a, b in route):
            piece = lax.ppermute(piece, "slab", route)
        arrived.append(piece)

    result = []
    for first, last, spot in zip(cuts[:-1], cuts[1:], spots):
        span = last - first
        result = [
            pl.pallas_call(
                functools.partial(join_kernel, span),
                grid_spec=pltpu.PrefetchScalarGridSpec(
                    num_scalar_prefetch=1,
                    grid=(span,),
                    in_specs=[vmem()] * (1 + span)
                    + [pl.BlockSpec(memory_space=pl.ANY)] * len(result),
                    out_specs=pl.BlockSpec(
                        (1, 2, vectors, width),
                        lambda i, at, span=span: (at[i], 0, at[span + i], 0),
                    ),
                ),
                out_shape=jax.ShapeDtypeStruct(perambulators.shape, bf16),
                input_output_aliases={2 + span: 0} if result else {},
                compiler_params=pltpu.CompilerParams(vmem_limit_bytes=6 << 20),
                name="join",
            )(spot, spread_spins, *arrived[first:last], *result)
        ]
    return result[0]


def solution(mesh):
    return jax.shard_map(
        body,
        mesh=mesh,
        in_specs=(
            P(("cfg", "tile"), None, None, "slab", "spin", None),
            P(("cfg", "tile"), None, None, None, "slab", "spin"),
            P(),
            P(),
            P("tile", None),
            P(("cfg", "tile"), None, "spin", "slab"),
        ),
        out_specs=P(("cfg", "tile"), None, "spin", "slab"),
        check_vma=False,
    )
```

```python
import functools
import math

import jax
import jax.numpy as jnp
from jax import lax
from jax.experimental import pallas as pl
from jax.experimental.pallas import tpu as pltpu
from jax.sharding import PartitionSpec as P


NS = 4
LY = 32
LZ = 32
COLORS = 3
COEFS = 24
CUTS = 2


def shift(x, axis, by):
    count = lax.axis_size(axis)
    return lax.ppermute(x, axis, [(i, (i + by) % count) for i in range(count)])


def swap(x, axis, distance):
    count = lax.axis_size(axis)
    return lax.ppermute(x, axis, [(i, i ^ distance) for i in range(count)])


def vmem():
    return pl.BlockSpec(memory_space=pltpu.VMEM)


def smem():
    return pl.BlockSpec(memory_space=pltpu.SMEM)


def edge_kernel(spots, fields_ref, *refs):
    *outs, taken = refs
    copies = []
    for out, chunk in zip(outs, spots):
        for at, (part, c) in enumerate(chunk):
            copies.append(
                pltpu.make_async_copy(
                    fields_ref.at[part, c, 0], out.at[at], taken.at[len(copies)]
                )
            )
    for copy in copies:
        copy.start()
    for copy in copies:
        copy.wait()


def field_kernel(meta_ref, fields_ref, links_ref, turns_ref, inner_ref, outer_ref, rotated, coefs_ref):
    planes, block, vectors = fields_ref.shape[2:]
    tile = 16

    @pl.when(pl.program_id(0) == 0)
    def _():
        inner_ref[...] = jnp.zeros_like(inner_ref)

    for plane in range(planes):
        rows = [links_ref[:, plane, :], turns_ref[:, plane, :]]
        rows.append(jnp.zeros((COEFS - sum(row.shape[0] for row in rows), block), jnp.float32))
        coefs_ref[plane] = jnp.concatenate(rows, axis=0).T

        def rows_step(step, carry):
            rows = pl.ds(pl.multiple_of(step * tile, tile), tile)
            coefs = coefs_ref[plane, rows, :]

            def coef(which):
                return coefs[:, which : which + 1]

            real = [fields_ref[0, c, plane, rows, :].astype(jnp.float32) for c in range(COLORS)]
            imag = [fields_ref[1, c, plane, rows, :].astype(jnp.float32) for c in range(COLORS)]
            for out in range(COLORS):
                local_real = None
                for c in range(COLORS):
                    link_real = coef(COLORS * c + out)
                    link_imag = coef(COLORS * COLORS + COLORS * c + out)
                    term_real = link_real * real[c] + link_imag * imag[c]
                    term_imag = link_real * imag[c] - link_imag * real[c]
                    local_real = term_real if local_real is None else local_real + term_real
                    local_imag = term_imag if c == 0 else local_imag + term_imag
                for slot in range(2):
                    turn_real = coef(2 * COLORS * COLORS + 2 * slot)
                    turn_imag = coef(2 * COLORS * COLORS + 2 * slot + 1)
                    at = 2 * slot * vectors
                    rotated[out, rows, at : at + vectors] = (
                        turn_real * local_real - turn_imag * local_imag
                    ).astype(jnp.bfloat16)
                    at += vectors
                    rotated[out, rows, at : at + vectors] = (
                        turn_real * local_imag + turn_imag * local_real
                    ).astype(jnp.bfloat16)
            return carry

        lax.fori_loop(0, block // tile, rows_step, 0)
        for c in range(COLORS):
            if plane + 1 < planes:
                ahead = jnp.concatenate(
                    [fields_ref[0, c, plane + 1], fields_ref[1, c, plane + 1]], axis=1
                )
                inner_ref[...] += lax.dot_general(
                    rotated[c], ahead, (((0,), (0,)), ((), ())), preferred_element_type=jnp.float32
                )
            else:
                outer_ref[c] = rotated[c].T


def most_kernel(outer_ref, inner_ref, first_ref, most_ref, total_ref):
    vectors = most_ref.shape[-1]
    for slot in range(2):
        at = 2 * slot * vectors
        totals = []
        for part in range(2):
            total = inner_ref[at : at + 2 * vectors, part * vectors : (part + 1) * vectors]
            for c in range(COLORS - part):
                total = total + jnp.dot(
                    outer_ref[c, at : at + 2 * vectors, :],
                    most_ref[COLORS * part + c - 1] if part + c else first_ref[0],
                    preferred_element_type=jnp.float32,
                )
            totals.append(total)
        total_ref[slot, 0] = totals[0][:vectors] + totals[1][vectors:]
        total_ref[slot, 1] = totals[0][vectors:] - totals[1][:vectors]


def last_kernel(normalize, meta_ref, outer_ref, total_ref, last_ref, keep_ref, send_ref):
    vectors = last_ref.shape[-1]
    for slot, out in ((1, send_ref), (0, keep_ref)):
        at = 2 * slot * vectors
        both = jnp.dot(
            outer_ref[0, at : at + 2 * vectors, :],
            last_ref[0],
            preferred_element_type=jnp.float32,
        )
        real = total_ref[slot, 0] + both[vectors:]
        imag = total_ref[slot, 1] - both[:vectors]
        out[meta_ref[1]] = (real * normalize).astype(out.dtype)
        out[1 - meta_ref[1]] = (imag * normalize).astype(out.dtype)


def deal_kernel(share, meta_ref, perams_ref, move_ref, *outs):
    spin_rows = perams_ref.shape[2]
    width = outs[0].shape[-1]
    for which, out in enumerate(outs):
        by, half = which // CUTS, which % CUTS
        item = (meta_ref[4] ^ by) // share
        for part in range(2):
            out[part] = jnp.dot(
                perams_ref[item // spin_rows, part, lax.rem(item, spin_rows)],
                move_ref[:, half * width : (half + 1) * width],
                preferred_element_type=jnp.float32,
            ).astype(jnp.bfloat16)


def block_kernel(slab, share, meta_ref, *refs):
    parts = refs[:4]
    chunks = refs[4 : 4 + slab]
    outs = refs[4 + slab : -2]
    table_ref, turned_ref = refs[-2:]
    vectors = parts[0].shape[0]
    per = vectors // slab
    core, parity, place = meta_ref[0], meta_ref[1], meta_ref[4]
    found = [piece[...].astype(jnp.float32) for piece in parts]

    def pick(elem):
        mine = core == elem
        first = jnp.where(mine, found[0], found[2])
        second = jnp.where(mine, found[1], found[3])
        real = jnp.where(parity == 0, first, second)
        imag = jnp.where(parity == 0, second, first)
        forward = meta_ref[5 + elem] == 1
        return (
            jnp.where(forward, real, real.T),
            jnp.where(forward, -imag, imag.T),
        )

    real, imag = pick(0)
    real, imag = real.astype(jnp.bfloat16), imag.astype(jnp.bfloat16)
    matrix = jnp.concatenate(
        [jnp.concatenate([real, -imag], axis=1), jnp.concatenate([imag, real], axis=1)], axis=0
    )
    spins = NS // CUTS
    columns = []
    for spin in range(spins):
        at = spin * per
        columns += [
            chunk[...].reshape(2 * vectors, spins * per)[:, at : at + per] for chunk in chunks
        ]
    spread = jnp.concatenate(columns, axis=1)
    left = jnp.dot(matrix, spread, preferred_element_type=jnp.float32).astype(jnp.bfloat16)
    width = vectors // share
    count = slab // share
    lane = lax.broadcasted_iota(jnp.int32, (per, width), 1) // per
    for part, value in enumerate(pick(1)):
        table_ref[...] = value
        for chunk in range(slab):
            row = pl.multiple_of((place ^ chunk) * per, per)
            rows = table_ref[pl.ds(row, per), :]
            turned = rows[:, :width]
            for group in range(1, share):
                turned = jnp.where(
                    lax.rem(place, share) == group,
                    rows[:, group * width : (group + 1) * width],
                    turned,
                )
            step = 1
            while step < count:
                down = pltpu.roll(turned, step * per, 1)
                up = pltpu.roll(turned, width - step * per, 1)
                moved = jnp.where((lane // step) % 2 == 0, up, down)
                turned = jnp.where((place // (share * step)) % 2 == 1, moved, turned)
                step *= 2
            turned_ref[chunk * per : (chunk + 1) * per, part * width : (part + 1) * width] = (
                turned
            )
    right = turned_ref[...].astype(jnp.bfloat16)
    reals, imags = [], []
    for spin in range(spins):
        both = jnp.dot(
            left[:, spin * vectors : (spin + 1) * vectors],
            right,
            preferred_element_type=jnp.float32,
        )
        reals.append(both[:vectors, :width] - both[vectors:, width:])
        imags.append(both[:vectors, width:] + both[vectors:, :width])
    for which, out in enumerate(outs):
        at = which * per
        for part, values in ((0, reals), (1, imags)):
            out[part] = jnp.concatenate(
                [value[:, at : at + per] for value in values], axis=1
            ).astype(jnp.bfloat16)


def join_kernel(count, place_ref, move_ref, *refs):
    out_ref = refs[-1]
    for which in range(count):

        @pl.when(pl.program_id(0) == which)
        def _():
            cuts = refs[which * CUTS : (which + 1) * CUTS]
            for part in range(2):
                piece = jnp.concatenate([cut[part] for cut in cuts], axis=1)
                out_ref[0, part] = jnp.dot(
                    piece, move_ref[...], preferred_element_type=jnp.float32
                ).astype(jnp.bfloat16)


def body(eigenvectors, gauge_links, momenta, displacement, slice_pairs, perambulators):
    bf16, f32, i32 = jnp.bfloat16, jnp.float32, jnp.int32
    fields = eigenvectors[0]
    links = gauge_links[0]
    planes, sites, vectors = fields.shape[2:]
    slab, tiles = lax.axis_size("slab"), lax.axis_size("tile")
    z, t, core = lax.axis_index("slab"), lax.axis_index("tile"), lax.axis_index("spin")
    z, t, core = z.astype(i32), t.astype(i32), core.astype(i32)
    lattice_x = planes * slab
    normalize = 1.0 / math.sqrt(3072 * lattice_x * LY * LZ)

    def edge(spots):
        return pl.pallas_call(
            functools.partial(edge_kernel, spots),
            in_specs=[pl.BlockSpec(memory_space=pl.ANY)],
            out_specs=[vmem()] * len(spots),
            out_shape=[
                jax.ShapeDtypeStruct((len(chunk), sites, vectors), bf16) for chunk in spots
            ],
            scratch_shapes=[pltpu.SemaphoreType.DMA((sum(map(len, spots)),))],
            compiler_params=pltpu.CompilerParams(vmem_limit_bytes=62 << 20),
            name="edge",
        )(fields)

    spots = [(part, c) for part in range(2) for c in range(COLORS)]
    (first,) = edge((spots[:1],))
    first = shift(first, "slab", -1)
    most, last = edge((spots[1:-1], spots[-1:]))
    most = shift(most, "slab", -1)
    last = shift(last, "slab", -1)

    forward = (displacement == 1).astype(i32)
    forward = jnp.where(core == 0, forward, forward[::-1])
    turns = jnp.where(core == 0, momenta, momenta[::-1])
    x_site = z * planes + jnp.arange(planes, dtype=i32)[None, :] + (1 - forward)[:, None]
    yz_site = core * sites + jnp.arange(sites, dtype=i32)
    wave_x = jnp.mod(turns[:, 0:1] * x_site, lattice_x)
    wave_y = jnp.mod(turns[:, 1:2] * (yz_site // LZ)[None, :], LY)
    wave_z = jnp.mod(turns[:, 2:3] * (yz_site % LZ)[None, :], LZ)
    number = (
        wave_x[:, :, None] * (LY * LZ)
        + (wave_y * (lattice_x * LZ) + wave_z * (lattice_x * LY))[:, None, :]
    )
    angle = number.astype(f32) * (2.0 * math.pi / (lattice_x * LY * LZ))
    sign = (2 * forward - 1).astype(f32)[:, None, None]
    turn = jnp.stack([jnp.cos(angle), jnp.sin(angle) * sign], axis=1)
    turn = turn.reshape(4, planes, sites)
    links = links.reshape(2 * COLORS * COLORS, planes, sites)

    parity = lax.rem(z, 2)
    pairs = perambulators.shape[0]
    spin_rows = perambulators.shape[2] // vectors
    width = perambulators.shape[3]
    items = pairs * spin_rows
    share = slab // items
    assert share * items == slab and (share * spin_rows) % 2 == 0
    chosen = slice_pairs[z // share // spin_rows]
    meta = jnp.stack([core, parity, chosen[0], chosen[1], z, displacement[0], displacement[1]])

    per = width // NS
    column = jnp.arange(width, dtype=i32)
    target = (column % NS) * per + column // NS
    gather_spins = (target[:, None] == column[None, :]).astype(bf16)
    spread_spins = (target[None, :] == column[:, None]).astype(bf16)
    count = slab // share

    def places(low, high):
        found = lax.rem(z, count) ^ jnp.arange(low, high, dtype=i32)
        return jnp.concatenate([found // spin_rows, lax.rem(found, spin_rows)])

    cuts = (0, count // 2, count)
    wanted = [
        lax.rem(t - slice_pairs[place // share // spin_rows, core] + tiles, tiles)
        for place in (z, z ^ 2)
    ]
    spots = [places(low, high) for low, high in zip(cuts[:-1], cuts[1:])]
    meta, turn, gather_spins, spread_spins, wanted, spots = lax.optimization_barrier(
        (meta, turn, gather_spins, spread_spins, wanted, spots)
    )

    block = min(sites, 256)
    inner, outer = pl.pallas_call(
        field_kernel,
        grid=(sites // block,),
        in_specs=[
            smem(),
            pl.BlockSpec((2, COLORS, planes, block, vectors), lambda i: (0, 0, 0, i, 0)),
            pl.BlockSpec((2 * COLORS * COLORS, planes, block), lambda i: (0, 0, i)),
            pl.BlockSpec((4, planes, block), lambda i: (0, 0, i)),
        ],
        out_specs=[
            pl.BlockSpec((4 * vectors, 2 * vectors), lambda i: (0, 0)),
            pl.BlockSpec((COLORS, 4 * vectors, block), lambda i: (0, 0, i)),
        ],
        out_shape=[
            jax.ShapeDtypeStruct((4 * vectors, 2 * vectors), f32),
            jax.ShapeDtypeStruct((COLORS, 4 * vectors, sites), bf16),
        ],
        scratch_shapes=[
            pltpu.VMEM((COLORS, block, 4 * vectors), bf16),
            pltpu.VMEM((planes, block, COEFS), f32),
        ],
        compiler_params=pltpu.CompilerParams(vmem_limit_bytes=15 << 20),
        name="fields",
    )(meta, fields, links, turn)

    blocks = pl.pallas_call(
        functools.partial(deal_kernel, share),
        in_specs=[smem(), vmem(), vmem()],
        out_specs=[vmem()] * (slab * CUTS),
        out_shape=[jax.ShapeDtypeStruct((2, vectors, width // CUTS), bf16)] * (slab * CUTS),
        compiler_params=pltpu.CompilerParams(vmem_limit_bytes=8 << 20),
        name="deal",
    )(meta, perambulators.reshape(pairs, 2, spin_rows, vectors, width), gather_spins)
    outer, *blocks = lax.optimization_barrier((outer, *blocks))

    total = pl.pallas_call(
        most_kernel,
        in_specs=[vmem()] * 4,
        out_specs=vmem(),
        out_shape=jax.ShapeDtypeStruct((2, 2, vectors, vectors), f32),
        compiler_params=pltpu.CompilerParams(vmem_limit_bytes=14 << 20),
        name="most",
    )(outer, inner, first, most)
    keep, send = pl.pallas_call(
        functools.partial(last_kernel, normalize),
        grid=(1,),
        in_specs=[
            smem(),
            pl.BlockSpec((1, 4 * vectors, sites), lambda i: (COLORS - 1, 0, 0)),
            vmem(),
            vmem(),
        ],
        out_specs=[vmem()] * 2,
        out_shape=[
            jax.ShapeDtypeStruct((2, vectors, vectors), f32),
            jax.ShapeDtypeStruct((2, vectors, vectors), bf16),
        ],
        compiler_params=pltpu.CompilerParams(vmem_limit_bytes=10 << 20),
        name="last",
    )(meta, outer, total, last)

    half = keep + swap(send, "spin", 1).astype(f32)
    quarter = half[0] + swap(half[1].astype(bf16), "slab", 1).astype(f32)
    distance = 4
    while distance < slab:
        quarter = quarter + swap(quarter.astype(bf16), "slab", distance).astype(f32)
        distance *= 2
    own, theirs = quarter, quarter.astype(bf16)
    for by in range(1, tiles):
        moved = shift(quarter.astype(bf16), "tile", by)
        own = jnp.where(wanted[0] == by, moved.astype(f32), own)
        theirs = jnp.where(wanted[1] == by, moved, theirs)
    own = (own + swap(theirs, "slab", 2).astype(f32)).astype(bf16)
    pair = swap(own, "slab", 1)
    own_core = swap(own, "spin", 1)
    pair_core = swap(pair, "spin", 1)

    pieces = []
    for cut in range(CUTS):
        chunks = [blocks[cut]]
        for by in range(1, slab):
            chunks.append(swap(blocks[by * CUTS + cut], "slab", by))
        found = pl.pallas_call(
            functools.partial(block_kernel, slab, share),
            in_specs=[smem()] + [vmem()] * (4 + slab),
            out_specs=[vmem()] * count,
            out_shape=[jax.ShapeDtypeStruct((2, vectors, width // CUTS), bf16)] * count,
            scratch_shapes=[
                pltpu.VMEM((vectors, vectors), f32),
                pltpu.VMEM((vectors, 2 * vectors // share), f32),
            ],
            compiler_params=pltpu.CompilerParams(vmem_limit_bytes=14 << 20),
            name="blocks",
        )(meta, own, pair, own_core, pair_core, *chunks)
        arrived = []
        for which, piece in enumerate(found):
            route = [(s, (s % share) * count + ((s // share) ^ which)) for s in range(slab)]
            if any(a != b for a, b in route):
                piece = lax.ppermute(piece, "slab", route)
            arrived.append(piece)
        pieces.append(arrived)

    result = []
    for low, high, spot in zip(cuts[:-1], cuts[1:], spots):
        span = high - low
        result = [
            pl.pallas_call(
                functools.partial(join_kernel, span),
                grid_spec=pltpu.PrefetchScalarGridSpec(
                    num_scalar_prefetch=1,
                    grid=(span,),
                    in_specs=[vmem()] * (1 + span * CUTS)
                    + [pl.BlockSpec(memory_space=pl.ANY)] * len(result),
                    out_specs=pl.BlockSpec(
                        (1, 2, vectors, width),
                        lambda i, at, span=span: (at[i], 0, at[span + i], 0),
                    ),
                ),
                out_shape=jax.ShapeDtypeStruct(perambulators.shape, bf16),
                input_output_aliases={2 + span * CUTS: 0} if result else {},
                compiler_params=pltpu.CompilerParams(vmem_limit_bytes=6 << 20),
                name="join",
            )(
                spot,
                spread_spins,
                *[arrived[at] for at in range(low, high) for arrived in pieces],
                *result,
            )
        ]
    return result[0]


def solution(mesh):
    return jax.shard_map(
        body,
        mesh=mesh,
        in_specs=(
            P(("cfg", "tile"), None, None, "slab", "spin", None),
            P(("cfg", "tile"), None, None, None, "slab", "spin"),
            P(),
            P(),
            P("tile", None),
            P(("cfg", "tile"), None, "spin", "slab"),
        ),
        out_specs=P(("cfg", "tile"), None, "spin", "slab"),
        check_vma=False,
    )
```

```python
import functools
import math

import jax
import jax.numpy as jnp
from jax import lax
from jax.experimental import pallas as pl
from jax.experimental.pallas import tpu as pltpu
from jax.sharding import PartitionSpec as P


NS = 4
LY = 32
LZ = 32
COLORS = 3
COEFS = 24
CUTS = 2


def shift(x, axis, by):
    count = lax.axis_size(axis)
    return lax.ppermute(x, axis, [(i, (i + by) % count) for i in range(count)])


def swap(x, axis, distance):
    count = lax.axis_size(axis)
    return lax.ppermute(x, axis, [(i, i ^ distance) for i in range(count)])


def vmem():
    return pl.BlockSpec(memory_space=pltpu.VMEM)


def smem():
    return pl.BlockSpec(memory_space=pltpu.SMEM)


def edge_kernel(spots, fields_ref, *refs):
    *outs, taken = refs
    copies = []
    for out, chunk in zip(outs, spots):
        for at, (part, c) in enumerate(chunk):
            copies.append(
                pltpu.make_async_copy(
                    fields_ref.at[part, c, 0], out.at[at], taken.at[len(copies)]
                )
            )
    for copy in copies:
        copy.start()
    for copy in copies:
        copy.wait()


def field_kernel(meta_ref, fields_ref, links_ref, turns_ref, inner_ref, outer_ref, rotated, coefs_ref):
    planes, block, vectors = fields_ref.shape[2:]
    tile = 16

    @pl.when(pl.program_id(0) == 0)
    def _():
        inner_ref[...] = jnp.zeros_like(inner_ref)

    for plane in range(planes):
        rows = [links_ref[:, plane, :], turns_ref[:, plane, :]]
        rows.append(jnp.zeros((COEFS - sum(row.shape[0] for row in rows), block), jnp.float32))
        coefs_ref[plane] = jnp.concatenate(rows, axis=0).T

        def rows_step(step, carry):
            rows = pl.ds(pl.multiple_of(step * tile, tile), tile)
            coefs = coefs_ref[plane, rows, :]

            def coef(which):
                return coefs[:, which : which + 1]

            real = [fields_ref[0, c, plane, rows, :].astype(jnp.float32) for c in range(COLORS)]
            imag = [fields_ref[1, c, plane, rows, :].astype(jnp.float32) for c in range(COLORS)]
            for out in range(COLORS):
                local_real = None
                for c in range(COLORS):
                    link_real = coef(COLORS * c + out)
                    link_imag = coef(COLORS * COLORS + COLORS * c + out)
                    term_real = link_real * real[c] + link_imag * imag[c]
                    term_imag = link_real * imag[c] - link_imag * real[c]
                    local_real = term_real if local_real is None else local_real + term_real
                    local_imag = term_imag if c == 0 else local_imag + term_imag
                for slot in range(2):
                    turn_real = coef(2 * COLORS * COLORS + 2 * slot)
                    turn_imag = coef(2 * COLORS * COLORS + 2 * slot + 1)
                    at = 2 * slot * vectors
                    rotated[out, rows, at : at + vectors] = (
                        turn_real * local_real - turn_imag * local_imag
                    ).astype(jnp.bfloat16)
                    at += vectors
                    rotated[out, rows, at : at + vectors] = (
                        turn_real * local_imag + turn_imag * local_real
                    ).astype(jnp.bfloat16)
            return carry

        lax.fori_loop(0, block // tile, rows_step, 0)
        for c in range(COLORS):
            if plane + 1 < planes:
                ahead = jnp.concatenate(
                    [fields_ref[0, c, plane + 1], fields_ref[1, c, plane + 1]], axis=1
                )
                inner_ref[...] += lax.dot_general(
                    rotated[c], ahead, (((0,), (0,)), ((), ())), preferred_element_type=jnp.float32
                )
            else:
                outer_ref[c] = rotated[c].T


def most_kernel(outer_ref, inner_ref, first_ref, most_ref, total_ref):
    vectors = most_ref.shape[-1]
    for slot in range(2):
        at = 2 * slot * vectors
        totals = []
        for part in range(2):
            total = inner_ref[at : at + 2 * vectors, part * vectors : (part + 1) * vectors]
            for c in range(COLORS - part):
                total = total + jnp.dot(
                    outer_ref[c, at : at + 2 * vectors, :],
                    most_ref[COLORS * part + c - 1] if part + c else first_ref[0],
                    preferred_element_type=jnp.float32,
                )
            totals.append(total)
        total_ref[slot, 0] = totals[0][:vectors] + totals[1][vectors:]
        total_ref[slot, 1] = totals[0][vectors:] - totals[1][:vectors]


def last_kernel(normalize, meta_ref, outer_ref, total_ref, last_ref, keep_ref, send_ref):
    vectors = last_ref.shape[-1]
    for slot, out in ((1, send_ref), (0, keep_ref)):
        at = 2 * slot * vectors
        both = jnp.dot(
            outer_ref[0, at : at + 2 * vectors, :],
            last_ref[0],
            preferred_element_type=jnp.float32,
        )
        real = total_ref[slot, 0] + both[vectors:]
        imag = total_ref[slot, 1] - both[:vectors]
        out[meta_ref[1]] = (real * normalize).astype(out.dtype)
        out[1 - meta_ref[1]] = (imag * normalize).astype(out.dtype)


def deal_kernel(share, meta_ref, perams_ref, move_ref, *outs):
    spin_rows = perams_ref.shape[2]
    width = outs[0].shape[-1]
    for which, out in enumerate(outs):
        by, half = which // CUTS, which % CUTS
        item = (meta_ref[4] ^ by) // share
        for part in range(2):
            out[part] = jnp.dot(
                perams_ref[item // spin_rows, part, lax.rem(item, spin_rows)],
                move_ref[:, half * width : (half + 1) * width],
                preferred_element_type=jnp.float32,
            ).astype(jnp.bfloat16)


def block_kernel(slab, share, meta_ref, *refs):
    parts = refs[:4]
    chunks = refs[4 : 4 + slab]
    outs = refs[4 + slab : -2]
    table_ref, turned_ref = refs[-2:]
    vectors = parts[0].shape[0]
    per = vectors // slab
    core, parity, place = meta_ref[0], meta_ref[1], meta_ref[4]
    found = [piece[...].astype(jnp.float32) for piece in parts]

    def pick(elem):
        mine = core == elem
        first = jnp.where(mine, found[0], found[2])
        second = jnp.where(mine, found[1], found[3])
        real = jnp.where(parity == 0, first, second)
        imag = jnp.where(parity == 0, second, first)
        forward = meta_ref[5 + elem] == 1
        return (
            jnp.where(forward, real, real.T),
            jnp.where(forward, -imag, imag.T),
        )

    real, imag = pick(0)
    real, imag = real.astype(jnp.bfloat16), imag.astype(jnp.bfloat16)
    matrix = jnp.concatenate(
        [jnp.concatenate([real, -imag], axis=1), jnp.concatenate([imag, real], axis=1)], axis=0
    )
    spins = NS // CUTS
    columns = []
    for spin in range(spins):
        at = spin * per
        columns += [
            chunk[...].reshape(2 * vectors, spins * per)[:, at : at + per] for chunk in chunks
        ]
    spread = jnp.concatenate(columns, axis=1)
    left = jnp.dot(matrix, spread, preferred_element_type=jnp.float32).astype(jnp.bfloat16)
    width = vectors // share
    count = slab // share
    lane = lax.broadcasted_iota(jnp.int32, (per, width), 1) // per
    for part, value in enumerate(pick(1)):
        table_ref[...] = value
        for chunk in range(slab):
            row = pl.multiple_of((place ^ chunk) * per, per)
            rows = table_ref[pl.ds(row, per), :]
            turned = rows[:, :width]
            for group in range(1, share):
                turned = jnp.where(
                    lax.rem(place, share) == group,
                    rows[:, group * width : (group + 1) * width],
                    turned,
                )
            step = 1
            while step < count:
                down = pltpu.roll(turned, step * per, 1)
                up = pltpu.roll(turned, width - step * per, 1)
                moved = jnp.where((lane // step) % 2 == 0, up, down)
                turned = jnp.where((place // (share * step)) % 2 == 1, moved, turned)
                step *= 2
            turned_ref[chunk * per : (chunk + 1) * per, part * width : (part + 1) * width] = (
                turned
            )
    right = turned_ref[...].astype(jnp.bfloat16)
    reals, imags = [], []
    for spin in range(spins):
        both = jnp.dot(
            left[:, spin * vectors : (spin + 1) * vectors],
            right,
            preferred_element_type=jnp.float32,
        )
        reals.append(both[:vectors, :width] - both[vectors:, width:])
        imags.append(both[:vectors, width:] + both[vectors:, :width])
    for which, out in enumerate(outs):
        at = which * per
        for part, values in ((0, reals), (1, imags)):
            out[part] = jnp.concatenate(
                [value[:, at : at + per] for value in values], axis=1
            ).astype(jnp.bfloat16)


def join_kernel(count, place_ref, move_ref, *refs):
    out_ref, joined, given = refs[-3:]
    vectors = joined.shape[2]
    copies = []
    for which in range(count):
        cuts = refs[which * CUTS : (which + 1) * CUTS]
        for part in range(2):
            piece = jnp.concatenate([cut[part] for cut in cuts], axis=1)
            joined[which, part] = jnp.dot(
                piece, move_ref[...], preferred_element_type=jnp.float32
            ).astype(jnp.bfloat16)
        row = pl.multiple_of(place_ref[count + which] * vectors, vectors)
        copies.append(
            pltpu.make_async_copy(
                joined.at[which],
                out_ref.at[place_ref[which], :, pl.ds(row, vectors), :],
                given.at[which],
            )
        )
        copies[-1].start()
    for copy in copies:
        copy.wait()


def body(eigenvectors, gauge_links, momenta, displacement, slice_pairs, perambulators):
    bf16, f32, i32 = jnp.bfloat16, jnp.float32, jnp.int32
    fields = eigenvectors[0]
    links = gauge_links[0]
    planes, sites, vectors = fields.shape[2:]
    slab, tiles = lax.axis_size("slab"), lax.axis_size("tile")
    z, t, core = lax.axis_index("slab"), lax.axis_index("tile"), lax.axis_index("spin")
    z, t, core = z.astype(i32), t.astype(i32), core.astype(i32)
    lattice_x = planes * slab
    normalize = 1.0 / math.sqrt(3072 * lattice_x * LY * LZ)

    def edge(spots):
        return pl.pallas_call(
            functools.partial(edge_kernel, spots),
            in_specs=[pl.BlockSpec(memory_space=pl.ANY)],
            out_specs=[vmem()] * len(spots),
            out_shape=[
                jax.ShapeDtypeStruct((len(chunk), sites, vectors), bf16) for chunk in spots
            ],
            scratch_shapes=[pltpu.SemaphoreType.DMA((sum(map(len, spots)),))],
            compiler_params=pltpu.CompilerParams(vmem_limit_bytes=62 << 20),
            name="edge",
        )(fields)

    spots = [(part, c) for part in range(2) for c in range(COLORS)]
    (first,) = edge((spots[:1],))
    first = shift(first, "slab", -1)
    most, last = edge((spots[1:-1], spots[-1:]))
    most = shift(most, "slab", -1)
    last = shift(last, "slab", -1)

    forward = (displacement == 1).astype(i32)
    forward = jnp.where(core == 0, forward, forward[::-1])
    turns = jnp.where(core == 0, momenta, momenta[::-1])
    x_site = z * planes + jnp.arange(planes, dtype=i32)[None, :] + (1 - forward)[:, None]
    yz_site = core * sites + jnp.arange(sites, dtype=i32)
    wave_x = jnp.mod(turns[:, 0:1] * x_site, lattice_x)
    wave_y = jnp.mod(turns[:, 1:2] * (yz_site // LZ)[None, :], LY)
    wave_z = jnp.mod(turns[:, 2:3] * (yz_site % LZ)[None, :], LZ)
    number = (
        wave_x[:, :, None] * (LY * LZ)
        + (wave_y * (lattice_x * LZ) + wave_z * (lattice_x * LY))[:, None, :]
    )
    angle = number.astype(f32) * (2.0 * math.pi / (lattice_x * LY * LZ))
    sign = (2 * forward - 1).astype(f32)[:, None, None]
    turn = jnp.stack([jnp.cos(angle), jnp.sin(angle) * sign], axis=1)
    turn = turn.reshape(4, planes, sites)
    links = links.reshape(2 * COLORS * COLORS, planes, sites)

    parity = lax.rem(z, 2)
    pairs = perambulators.shape[0]
    spin_rows = perambulators.shape[2] // vectors
    width = perambulators.shape[3]
    items = pairs * spin_rows
    share = slab // items
    assert share * items == slab and (share * spin_rows) % 2 == 0
    chosen = slice_pairs[z // share // spin_rows]
    meta = jnp.stack([core, parity, chosen[0], chosen[1], z, displacement[0], displacement[1]])

    per = width // NS
    column = jnp.arange(width, dtype=i32)
    target = (column % NS) * per + column // NS
    gather_spins = (target[:, None] == column[None, :]).astype(bf16)
    spread_spins = (target[None, :] == column[:, None]).astype(bf16)
    count = slab // share

    def places(low, high):
        found = lax.rem(z, count) ^ jnp.arange(low, high, dtype=i32)
        return jnp.concatenate([found // spin_rows, lax.rem(found, spin_rows)])

    cuts = (0, count // 2, count)
    wanted = [
        lax.rem(t - slice_pairs[place // share // spin_rows, core] + tiles, tiles)
        for place in (z, z ^ 2)
    ]
    spots = [places(low, high) for low, high in zip(cuts[:-1], cuts[1:])]
    meta, turn, gather_spins, spread_spins, wanted, spots = lax.optimization_barrier(
        (meta, turn, gather_spins, spread_spins, wanted, spots)
    )

    block = min(sites, 256)
    inner, outer = pl.pallas_call(
        field_kernel,
        grid=(sites // block,),
        in_specs=[
            smem(),
            pl.BlockSpec((2, COLORS, planes, block, vectors), lambda i: (0, 0, 0, i, 0)),
            pl.BlockSpec((2 * COLORS * COLORS, planes, block), lambda i: (0, 0, i)),
            pl.BlockSpec((4, planes, block), lambda i: (0, 0, i)),
        ],
        out_specs=[
            pl.BlockSpec((4 * vectors, 2 * vectors), lambda i: (0, 0)),
            pl.BlockSpec((COLORS, 4 * vectors, block), lambda i: (0, 0, i)),
        ],
        out_shape=[
            jax.ShapeDtypeStruct((4 * vectors, 2 * vectors), f32),
            jax.ShapeDtypeStruct((COLORS, 4 * vectors, sites), bf16),
        ],
        scratch_shapes=[
            pltpu.VMEM((COLORS, block, 4 * vectors), bf16),
            pltpu.VMEM((planes, block, COEFS), f32),
        ],
        compiler_params=pltpu.CompilerParams(vmem_limit_bytes=15 << 20),
        name="fields",
    )(meta, fields, links, turn)

    blocks = pl.pallas_call(
        functools.partial(deal_kernel, share),
        in_specs=[smem(), vmem(), vmem()],
        out_specs=[vmem()] * (slab * CUTS),
        out_shape=[jax.ShapeDtypeStruct((2, vectors, width // CUTS), bf16)] * (slab * CUTS),
        compiler_params=pltpu.CompilerParams(vmem_limit_bytes=8 << 20),
        name="deal",
    )(meta, perambulators.reshape(pairs, 2, spin_rows, vectors, width), gather_spins)
    outer, *blocks = lax.optimization_barrier((outer, *blocks))

    total = pl.pallas_call(
        most_kernel,
        in_specs=[vmem()] * 4,
        out_specs=vmem(),
        out_shape=jax.ShapeDtypeStruct((2, 2, vectors, vectors), f32),
        compiler_params=pltpu.CompilerParams(vmem_limit_bytes=14 << 20),
        name="most",
    )(outer, inner, first, most)
    keep, send = pl.pallas_call(
        functools.partial(last_kernel, normalize),
        grid=(1,),
        in_specs=[
            smem(),
            pl.BlockSpec((1, 4 * vectors, sites), lambda i: (COLORS - 1, 0, 0)),
            vmem(),
            vmem(),
        ],
        out_specs=[vmem()] * 2,
        out_shape=[
            jax.ShapeDtypeStruct((2, vectors, vectors), f32),
            jax.ShapeDtypeStruct((2, vectors, vectors), bf16),
        ],
        compiler_params=pltpu.CompilerParams(vmem_limit_bytes=10 << 20),
        name="last",
    )(meta, outer, total, last)

    half = keep + swap(send, "spin", 1).astype(f32)
    quarter = half[0] + swap(half[1].astype(bf16), "slab", 1).astype(f32)
    distance = 4
    while distance < slab:
        quarter = quarter + swap(quarter.astype(bf16), "slab", distance).astype(f32)
        distance *= 2
    own, theirs = quarter, quarter.astype(bf16)
    for by in range(1, tiles):
        moved = shift(quarter.astype(bf16), "tile", by)
        own = jnp.where(wanted[0] == by, moved.astype(f32), own)
        theirs = jnp.where(wanted[1] == by, moved, theirs)
    own = (own + swap(theirs, "slab", 2).astype(f32)).astype(bf16)
    pair = swap(own, "slab", 1)
    own_core = swap(own, "spin", 1)
    pair_core = swap(pair, "spin", 1)

    pieces = []
    for cut in range(CUTS):
        chunks = [blocks[cut]]
        for by in range(1, slab):
            chunks.append(swap(blocks[by * CUTS + cut], "slab", by))
        found = pl.pallas_call(
            functools.partial(block_kernel, slab, share),
            in_specs=[smem()] + [vmem()] * (4 + slab),
            out_specs=[vmem()] * count,
            out_shape=[jax.ShapeDtypeStruct((2, vectors, width // CUTS), bf16)] * count,
            scratch_shapes=[
                pltpu.VMEM((vectors, vectors), f32),
                pltpu.VMEM((vectors, 2 * vectors // share), f32),
            ],
            compiler_params=pltpu.CompilerParams(vmem_limit_bytes=14 << 20),
            name="blocks",
        )(meta, own, pair, own_core, pair_core, *chunks)
        arrived = []
        for which, piece in enumerate(found):
            route = [(s, (s % share) * count + ((s // share) ^ which)) for s in range(slab)]
            if any(a != b for a, b in route):
                piece = lax.ppermute(piece, "slab", route)
            arrived.append(piece)
        pieces.append(arrived)

    result = []
    for low, high, spot in zip(cuts[:-1], cuts[1:], spots):
        span = high - low
        result = [
            pl.pallas_call(
                functools.partial(join_kernel, span),
                in_specs=[smem()]
                + [vmem()] * (1 + span * CUTS)
                + [pl.BlockSpec(memory_space=pl.ANY)] * len(result),
                out_specs=pl.BlockSpec(memory_space=pl.ANY),
                out_shape=jax.ShapeDtypeStruct(perambulators.shape, bf16),
                scratch_shapes=[
                    pltpu.VMEM((span, 2, vectors, width), bf16),
                    pltpu.SemaphoreType.DMA((span,)),
                ],
                input_output_aliases={2 + span * CUTS: 0} if result else {},
                compiler_params=pltpu.CompilerParams(vmem_limit_bytes=6 << 20),
                name="join",
            )(
                spot,
                spread_spins,
                *[arrived[at] for at in range(low, high) for arrived in pieces],
                *result,
            )
        ]
    return result[0]


def solution(mesh):
    return jax.shard_map(
        body,
        mesh=mesh,
        in_specs=(
            P(("cfg", "tile"), None, None, "slab", "spin", None),
            P(("cfg", "tile"), None, None, None, "slab", "spin"),
            P(),
            P(),
            P("tile", None),
            P(("cfg", "tile"), None, "spin", "slab"),
        ),
        out_specs=P(("cfg", "tile"), None, "spin", "slab"),
        check_vma=False,
    )
```

```python
import functools
import math

import jax
import jax.numpy as jnp
from jax import lax
from jax.experimental import pallas as pl
from jax.experimental.pallas import tpu as pltpu
from jax.sharding import PartitionSpec as P


NS = 4
LY = 32
LZ = 32
COLORS = 3
COEFS = 24
CUTS = 2


def shift(x, axis, by):
    count = lax.axis_size(axis)
    return lax.ppermute(x, axis, [(i, (i + by) % count) for i in range(count)])


def swap(x, axis, distance):
    count = lax.axis_size(axis)
    return lax.ppermute(x, axis, [(i, i ^ distance) for i in range(count)])


def vmem():
    return pl.BlockSpec(memory_space=pltpu.VMEM)


def smem():
    return pl.BlockSpec(memory_space=pltpu.SMEM)


def edge_kernel(spots, fields_ref, *refs):
    *outs, taken = refs
    copies = []
    for out, chunk in zip(outs, spots):
        for at, (part, c) in enumerate(chunk):
            copies.append(
                pltpu.make_async_copy(
                    fields_ref.at[part, c, 0], out.at[at], taken.at[len(copies)]
                )
            )
    for copy in copies:
        copy.start()
    for copy in copies:
        copy.wait()


def field_kernel(meta_ref, fields_ref, links_ref, turns_ref, inner_ref, outer_ref, rotated, coefs_ref):
    planes, block, vectors = fields_ref.shape[2:]
    tile = 16

    @pl.when(pl.program_id(0) == 0)
    def _():
        inner_ref[...] = jnp.zeros_like(inner_ref)

    for plane in range(planes):
        rows = [links_ref[:, plane, :], turns_ref[:, plane, :]]
        rows.append(jnp.zeros((COEFS - sum(row.shape[0] for row in rows), block), jnp.float32))
        coefs_ref[plane] = jnp.concatenate(rows, axis=0).T

        def rows_step(step, carry):
            rows = pl.ds(pl.multiple_of(step * tile, tile), tile)
            coefs = coefs_ref[plane, rows, :]

            def coef(which):
                return coefs[:, which : which + 1]

            real = [fields_ref[0, c, plane, rows, :].astype(jnp.float32) for c in range(COLORS)]
            imag = [fields_ref[1, c, plane, rows, :].astype(jnp.float32) for c in range(COLORS)]
            for out in range(COLORS):
                local_real = None
                for c in range(COLORS):
                    link_real = coef(COLORS * c + out)
                    link_imag = coef(COLORS * COLORS + COLORS * c + out)
                    term_real = link_real * real[c] + link_imag * imag[c]
                    term_imag = link_real * imag[c] - link_imag * real[c]
                    local_real = term_real if local_real is None else local_real + term_real
                    local_imag = term_imag if c == 0 else local_imag + term_imag
                for slot in range(2):
                    turn_real = coef(2 * COLORS * COLORS + 2 * slot)
                    turn_imag = coef(2 * COLORS * COLORS + 2 * slot + 1)
                    at = 2 * slot * vectors
                    rotated[out, rows, at : at + vectors] = (
                        turn_real * local_real - turn_imag * local_imag
                    ).astype(jnp.bfloat16)
                    at += vectors
                    rotated[out, rows, at : at + vectors] = (
                        turn_real * local_imag + turn_imag * local_real
                    ).astype(jnp.bfloat16)
            return carry

        lax.fori_loop(0, block // tile, rows_step, 0)
        for c in range(COLORS):
            if plane + 1 < planes:
                ahead = jnp.concatenate(
                    [fields_ref[0, c, plane + 1], fields_ref[1, c, plane + 1]], axis=1
                )
                inner_ref[...] += lax.dot_general(
                    rotated[c], ahead, (((0,), (0,)), ((), ())), preferred_element_type=jnp.float32
                )
            else:
                outer_ref[c] = rotated[c].T


def most_kernel(outer_ref, inner_ref, first_ref, most_ref, total_ref):
    vectors = most_ref.shape[-1]
    for slot in range(2):
        at = 2 * slot * vectors
        totals = []
        for part in range(2):
            total = inner_ref[at : at + 2 * vectors, part * vectors : (part + 1) * vectors]
            for c in range(COLORS - part):
                total = total + jnp.dot(
                    outer_ref[c, at : at + 2 * vectors, :],
                    most_ref[COLORS * part + c - 1] if part + c else first_ref[0],
                    preferred_element_type=jnp.float32,
                )
            totals.append(total)
        total_ref[slot, 0] = totals[0][:vectors] + totals[1][vectors:]
        total_ref[slot, 1] = totals[0][vectors:] - totals[1][:vectors]


def last_kernel(normalize, slot, meta_ref, outer_ref, total_ref, last_ref, out_ref):
    vectors = last_ref.shape[-1]
    both = jnp.dot(outer_ref[0], last_ref[0], preferred_element_type=jnp.float32)
    real = total_ref[slot, 0] + both[vectors:]
    imag = total_ref[slot, 1] - both[:vectors]
    out_ref[meta_ref[1]] = (real * normalize).astype(out_ref.dtype)
    out_ref[1 - meta_ref[1]] = (imag * normalize).astype(out_ref.dtype)


def deal_kernel(share, meta_ref, perams_ref, move_ref, *outs):
    spin_rows = perams_ref.shape[2]
    width = outs[0].shape[-1]
    for which, out in enumerate(outs):
        by, half = which // CUTS, which % CUTS
        item = (meta_ref[4] ^ by) // share
        for part in range(2):
            out[part] = jnp.dot(
                perams_ref[item // spin_rows, part, lax.rem(item, spin_rows)],
                move_ref[:, half * width : (half + 1) * width],
                preferred_element_type=jnp.float32,
            ).astype(jnp.bfloat16)


def block_kernel(slab, share, meta_ref, *refs):
    parts = refs[:4]
    chunks = refs[4 : 4 + slab]
    outs = refs[4 + slab : -2]
    table_ref, turned_ref = refs[-2:]
    vectors = parts[0].shape[0]
    per = vectors // slab
    core, parity, place = meta_ref[0], meta_ref[1], meta_ref[4]
    found = [piece[...].astype(jnp.float32) for piece in parts]

    def pick(elem):
        mine = core == elem
        first = jnp.where(mine, found[0], found[2])
        second = jnp.where(mine, found[1], found[3])
        real = jnp.where(parity == 0, first, second)
        imag = jnp.where(parity == 0, second, first)
        forward = meta_ref[5 + elem] == 1
        return (
            jnp.where(forward, real, real.T),
            jnp.where(forward, -imag, imag.T),
        )

    real, imag = pick(0)
    real, imag = real.astype(jnp.bfloat16), imag.astype(jnp.bfloat16)
    matrix = jnp.concatenate(
        [jnp.concatenate([real, -imag], axis=1), jnp.concatenate([imag, real], axis=1)], axis=0
    )
    spins = NS // CUTS
    columns = []
    for spin in range(spins):
        at = spin * per
        columns += [
            chunk[...].reshape(2 * vectors, spins * per)[:, at : at + per] for chunk in chunks
        ]
    spread = jnp.concatenate(columns, axis=1)
    left = jnp.dot(matrix, spread, preferred_element_type=jnp.float32).astype(jnp.bfloat16)
    width = vectors // share
    count = slab // share
    lane = lax.broadcasted_iota(jnp.int32, (per, width), 1) // per
    for part, value in enumerate(pick(1)):
        table_ref[...] = value
        for chunk in range(slab):
            row = pl.multiple_of((place ^ chunk) * per, per)
            rows = table_ref[pl.ds(row, per), :]
            turned = rows[:, :width]
            for group in range(1, share):
                turned = jnp.where(
                    lax.rem(place, share) == group,
                    rows[:, group * width : (group + 1) * width],
                    turned,
                )
            step = 1
            while step < count:
                down = pltpu.roll(turned, step * per, 1)
                up = pltpu.roll(turned, width - step * per, 1)
                moved = jnp.where((lane // step) % 2 == 0, up, down)
                turned = jnp.where((place // (share * step)) % 2 == 1, moved, turned)
                step *= 2
            turned_ref[chunk * per : (chunk + 1) * per, part * width : (part + 1) * width] = (
                turned
            )
    right = turned_ref[...].astype(jnp.bfloat16)
    reals, imags = [], []
    for spin in range(spins):
        both = jnp.dot(
            left[:, spin * vectors : (spin + 1) * vectors],
            right,
            preferred_element_type=jnp.float32,
        )
        reals.append(both[:vectors, :width] - both[vectors:, width:])
        imags.append(both[:vectors, width:] + both[vectors:, :width])
    for which, out in enumerate(outs):
        at = which * per
        for part, values in ((0, reals), (1, imags)):
            out[part] = jnp.concatenate(
                [value[:, at : at + per] for value in values], axis=1
            ).astype(jnp.bfloat16)


def join_kernel(count, place_ref, move_ref, *refs):
    out_ref, joined, given = refs[-3:]
    vectors = joined.shape[2]
    copies = []
    for which in range(count):
        cuts = refs[which * CUTS : (which + 1) * CUTS]
        for part in range(2):
            piece = jnp.concatenate([cut[part] for cut in cuts], axis=1)
            joined[which, part] = jnp.dot(
                piece, move_ref[...], preferred_element_type=jnp.float32
            ).astype(jnp.bfloat16)
        row = pl.multiple_of(place_ref[count + which] * vectors, vectors)
        copies.append(
            pltpu.make_async_copy(
                joined.at[which],
                out_ref.at[place_ref[which], :, pl.ds(row, vectors), :],
                given.at[which],
            )
        )
        copies[-1].start()
    for copy in copies:
        copy.wait()


def body(eigenvectors, gauge_links, momenta, displacement, slice_pairs, perambulators):
    bf16, f32, i32 = jnp.bfloat16, jnp.float32, jnp.int32
    fields = eigenvectors[0]
    links = gauge_links[0]
    planes, sites, vectors = fields.shape[2:]
    slab, tiles = lax.axis_size("slab"), lax.axis_size("tile")
    z, t, core = lax.axis_index("slab"), lax.axis_index("tile"), lax.axis_index("spin")
    z, t, core = z.astype(i32), t.astype(i32), core.astype(i32)
    lattice_x = planes * slab
    normalize = 1.0 / math.sqrt(3072 * lattice_x * LY * LZ)

    def edge(spots):
        return pl.pallas_call(
            functools.partial(edge_kernel, spots),
            in_specs=[pl.BlockSpec(memory_space=pl.ANY)],
            out_specs=[vmem()] * len(spots),
            out_shape=[
                jax.ShapeDtypeStruct((len(chunk), sites, vectors), bf16) for chunk in spots
            ],
            scratch_shapes=[pltpu.SemaphoreType.DMA((sum(map(len, spots)),))],
            compiler_params=pltpu.CompilerParams(vmem_limit_bytes=62 << 20),
            name="edge",
        )(fields)

    spots = [(part, c) for part in range(2) for c in range(COLORS)]
    (first,) = edge((spots[:1],))
    first = shift(first, "slab", -1)
    most, last = edge((spots[1:-1], spots[-1:]))
    most = shift(most, "slab", -1)
    last = shift(last, "slab", -1)

    forward = (displacement == 1).astype(i32)
    forward = jnp.where(core == 0, forward, forward[::-1])
    turns = jnp.where(core == 0, momenta, momenta[::-1])
    x_site = z * planes + jnp.arange(planes, dtype=i32)[None, :] + (1 - forward)[:, None]
    yz_site = core * sites + jnp.arange(sites, dtype=i32)
    wave_x = jnp.mod(turns[:, 0:1] * x_site, lattice_x)
    wave_y = jnp.mod(turns[:, 1:2] * (yz_site // LZ)[None, :], LY)
    wave_z = jnp.mod(turns[:, 2:3] * (yz_site % LZ)[None, :], LZ)
    number = (
        wave_x[:, :, None] * (LY * LZ)
        + (wave_y * (lattice_x * LZ) + wave_z * (lattice_x * LY))[:, None, :]
    )
    angle = number.astype(f32) * (2.0 * math.pi / (lattice_x * LY * LZ))
    sign = (2 * forward - 1).astype(f32)[:, None, None]
    turn = jnp.stack([jnp.cos(angle), jnp.sin(angle) * sign], axis=1)
    turn = turn.reshape(4, planes, sites)
    links = links.reshape(2 * COLORS * COLORS, planes, sites)

    parity = lax.rem(z, 2)
    pairs = perambulators.shape[0]
    spin_rows = perambulators.shape[2] // vectors
    width = perambulators.shape[3]
    items = pairs * spin_rows
    share = slab // items
    assert share * items == slab and (share * spin_rows) % 2 == 0
    chosen = slice_pairs[z // share // spin_rows]
    meta = jnp.stack([core, parity, chosen[0], chosen[1], z, displacement[0], displacement[1]])

    per = width // NS
    column = jnp.arange(width, dtype=i32)
    target = (column % NS) * per + column // NS
    gather_spins = (target[:, None] == column[None, :]).astype(bf16)
    spread_spins = (target[None, :] == column[:, None]).astype(bf16)
    count = slab // share

    def places(low, high):
        found = lax.rem(z, count) ^ jnp.arange(low, high, dtype=i32)
        return jnp.concatenate([found // spin_rows, lax.rem(found, spin_rows)])

    cuts = (0, count // 2, count)
    wanted = [
        lax.rem(t - slice_pairs[place // share // spin_rows, core] + tiles, tiles)
        for place in (z, z ^ 2)
    ]
    spots = [places(low, high) for low, high in zip(cuts[:-1], cuts[1:])]
    meta, turn, gather_spins, spread_spins, wanted, spots = lax.optimization_barrier(
        (meta, turn, gather_spins, spread_spins, wanted, spots)
    )

    block = min(sites, 256)
    inner, outer = pl.pallas_call(
        field_kernel,
        grid=(sites // block,),
        in_specs=[
            smem(),
            pl.BlockSpec((2, COLORS, planes, block, vectors), lambda i: (0, 0, 0, i, 0)),
            pl.BlockSpec((2 * COLORS * COLORS, planes, block), lambda i: (0, 0, i)),
            pl.BlockSpec((4, planes, block), lambda i: (0, 0, i)),
        ],
        out_specs=[
            pl.BlockSpec((4 * vectors, 2 * vectors), lambda i: (0, 0)),
            pl.BlockSpec((COLORS, 4 * vectors, block), lambda i: (0, 0, i)),
        ],
        out_shape=[
            jax.ShapeDtypeStruct((4 * vectors, 2 * vectors), f32),
            jax.ShapeDtypeStruct((COLORS, 4 * vectors, sites), bf16),
        ],
        scratch_shapes=[
            pltpu.VMEM((COLORS, block, 4 * vectors), bf16),
            pltpu.VMEM((planes, block, COEFS), f32),
        ],
        compiler_params=pltpu.CompilerParams(vmem_limit_bytes=15 << 20),
        name="fields",
    )(meta, fields, links, turn)

    blocks = pl.pallas_call(
        functools.partial(deal_kernel, share),
        in_specs=[smem(), vmem(), vmem()],
        out_specs=[vmem()] * (slab * CUTS),
        out_shape=[jax.ShapeDtypeStruct((2, vectors, width // CUTS), bf16)] * (slab * CUTS),
        compiler_params=pltpu.CompilerParams(vmem_limit_bytes=8 << 20),
        name="deal",
    )(meta, perambulators.reshape(pairs, 2, spin_rows, vectors, width), gather_spins)
    outer, *blocks = lax.optimization_barrier((outer, *blocks))

    total = pl.pallas_call(
        most_kernel,
        in_specs=[vmem()] * 4,
        out_specs=vmem(),
        out_shape=jax.ShapeDtypeStruct((2, 2, vectors, vectors), f32),
        compiler_params=pltpu.CompilerParams(vmem_limit_bytes=14 << 20),
        name="most",
    )(outer, inner, first, most)

    def finish(slot, dtype):
        return pl.pallas_call(
            functools.partial(last_kernel, normalize, slot),
            grid=(1,),
            in_specs=[
                smem(),
                pl.BlockSpec((1, 2 * vectors, sites), lambda i: (COLORS - 1, slot, 0)),
                vmem(),
                vmem(),
            ],
            out_specs=vmem(),
            out_shape=jax.ShapeDtypeStruct((2, vectors, vectors), dtype),
            compiler_params=pltpu.CompilerParams(vmem_limit_bytes=8 << 20),
            name="last",
        )(meta, outer, total, last)

    send = finish(1, bf16)
    keep = finish(0, f32)
    half = keep + swap(send, "spin", 1).astype(f32)
    quarter = half[0] + swap(half[1].astype(bf16), "slab", 1).astype(f32)
    distance = 4
    while distance < slab:
        quarter = quarter + swap(quarter.astype(bf16), "slab", distance).astype(f32)
        distance *= 2
    own, theirs = quarter, quarter.astype(bf16)
    for by in range(1, tiles):
        moved = shift(quarter.astype(bf16), "tile", by)
        own = jnp.where(wanted[0] == by, moved.astype(f32), own)
        theirs = jnp.where(wanted[1] == by, moved, theirs)
    own = (own + swap(theirs, "slab", 2).astype(f32)).astype(bf16)
    pair = swap(own, "slab", 1)
    own_core = swap(own, "spin", 1)
    pair_core = swap(pair, "spin", 1)

    pieces = []
    for cut in range(CUTS):
        chunks = [blocks[cut]]
        for by in range(1, slab):
            chunks.append(swap(blocks[by * CUTS + cut], "slab", by))
        found = pl.pallas_call(
            functools.partial(block_kernel, slab, share),
            in_specs=[smem()] + [vmem()] * (4 + slab),
            out_specs=[vmem()] * count,
            out_shape=[jax.ShapeDtypeStruct((2, vectors, width // CUTS), bf16)] * count,
            scratch_shapes=[
                pltpu.VMEM((vectors, vectors), f32),
                pltpu.VMEM((vectors, 2 * vectors // share), f32),
            ],
            compiler_params=pltpu.CompilerParams(vmem_limit_bytes=14 << 20),
            name="blocks",
        )(meta, own, pair, own_core, pair_core, *chunks)
        arrived = []
        for which, piece in enumerate(found):
            route = [(s, (s % share) * count + ((s // share) ^ which)) for s in range(slab)]
            if any(a != b for a, b in route):
                piece = lax.ppermute(piece, "slab", route)
            arrived.append(piece)
        pieces.append(arrived)

    result = []
    for low, high, spot in zip(cuts[:-1], cuts[1:], spots):
        span = high - low
        result = [
            pl.pallas_call(
                functools.partial(join_kernel, span),
                in_specs=[smem()]
                + [vmem()] * (1 + span * CUTS)
                + [pl.BlockSpec(memory_space=pl.ANY)] * len(result),
                out_specs=pl.BlockSpec(memory_space=pl.ANY),
                out_shape=jax.ShapeDtypeStruct(perambulators.shape, bf16),
                scratch_shapes=[
                    pltpu.VMEM((span, 2, vectors, width), bf16),
                    pltpu.SemaphoreType.DMA((span,)),
                ],
                input_output_aliases={2 + span * CUTS: 0} if result else {},
                compiler_params=pltpu.CompilerParams(vmem_limit_bytes=6 << 20),
                name="join",
            )(
                spot,
                spread_spins,
                *[arrived[at] for at in range(low, high) for arrived in pieces],
                *result,
            )
        ]
    return result[0]


def solution(mesh):
    return jax.shard_map(
        body,
        mesh=mesh,
        in_specs=(
            P(("cfg", "tile"), None, None, "slab", "spin", None),
            P(("cfg", "tile"), None, None, None, "slab", "spin"),
            P(),
            P(),
            P("tile", None),
            P(("cfg", "tile"), None, "spin", "slab"),
        ),
        out_specs=P(("cfg", "tile"), None, "spin", "slab"),
        check_vma=False,
    )
```
